32 devices in a mesh: row: 8 (over z, x), col: 4 (over y, core).
Axes of the slice: x: 2, y: 2, z: 4, core: 2. Of those that a mesh axis runs over, the one named last changes fastest.
Arguments:
- inputs: bfloat16 [4, 2048, 768], P(None, ('row', 'col')), may hold values from -6 to 6
- cotangent: bfloat16 [4, 2048, 768], P(None, ('row', 'col')), may hold values from -16 to 16
- projector: bfloat16 [768, 2304], P('row', 'col'), may hold values from -0.21875 to 0.21875
- projector_bias: bfloat16 [2304], P('col'), may hold values from -2 to 2
- combiner: bfloat16 [768, 768], P('row', 'col'), may hold values from -6 to 6
- combiner_bias: float32 [768], replicated, may hold values from -2 to 2
- attend_gain: float32 [768], replicated, may hold values from 0.5 to 1.5
- attend_shift: float32 [768], replicated, may hold values from -2 to 2
- expander: bfloat16 [768, 3072], P('row', 'col'), may hold values from -0.21875 to 0.21875
- expander_bias: bfloat16 [3072], P('col'), may hold values from -2 to 2
- reducer: bfloat16 [3072, 768], P('col', 'row'), may hold values from -0.109375 to 0.109375
- reducer_bias: float32 [768], replicated, may hold values from -2 to 2
- final_gain: float32 [768], replicated, may hold values from 0.5 to 1.5
- final_shift: float32 [768], replicated, may hold values from -2 to 2
- projection: float32 [256, 64], replicated, may hold values from -4 to 4
- lengths: int32 [4], replicated, may hold values from 512 to 2048, as said below
Outputs:
- layer_output: bfloat16 [4, 2048, 768], P(None, ('row', 'col'))
- input_gradient: float32 [4, 2048, 768], P(None, ('row', 'col'))
- grad_projector: float32 [768, 2304], P('row', 'col')
- grad_projector_bias: float32 [2304], P('col')
- grad_combiner: float32 [768, 768], P('row', 'col')
- grad_combiner_bias: float32 [768], replicated
- grad_attend_gain: float32 [768], replicated
- grad_attend_shift: float32 [768], replicated
- grad_expander: float32 [768, 3072], P('row', 'col')
- grad_expander_bias: float32 [3072], P('col')
- grad_reducer: float32 [3072, 768], P('col', 'row')
- grad_reducer_bias: float32 [768], replicated
- grad_final_gain: float32 [768], replicated
- grad_final_shift: float32 [768], replicated
The draws below stay inside these ranges and needn't reach their ends.
Inputs may be any that keep to these rules, and one draw needn't show every extreme that they name: `lengths`: slots at or past a sequence's length are padding. One sequence has 2048 valid slots and one has 512.
All inputs are finite; a program needn't handle non-finite values.
Results may differ from the reference program's by a relative error of at most 0.018.
Values may be sent and summed in bfloat16 or wider, within the bound.
No kernel may reach another device: no remote copies, remote signals or barrier semaphores. Data moves between devices by JAX's collectives and lax.ppermute only.
A program may use at most 192 MiB of HBM per device.

```python
import jax
import jax.numpy as jnp
from jax import lax

D = 768
H = 12
DH = 64
FF = 3072
M = 256
MICRO = 4
MB_SEQS = 1
SEQ = 2048
MBT = 2048
MIN_LEN = 512


def draw_cotangent(key, part):
    ranks = jnp.arange(MBT, dtype=jnp.float32) / (MBT - 1)
    drawn = jnp.clip(jax.random.normal(key, (MICRO, MBT, D), jnp.float32), -5.0, 5.0)
    scales = 1.0 + 2.0 * ranks
    return (drawn * scales[None, :, None]).astype(jnp.bfloat16)


def draw_lengths(key, part):
    slot_total = MICRO * MB_SEQS
    drawn = jax.random.randint(jax.random.fold_in(key, 1), (slot_total,), MIN_LEN, SEQ + 1, dtype=jnp.int32)
    picked = jax.random.permutation(jax.random.fold_in(key, 2), slot_total)
    drawn = drawn.at[picked[0]].set(SEQ)
    return drawn.at[picked[1]].set(MIN_LEN)


def shard_levels(rng, dims, cuts, least, top_value):
    loudness, own = 1.0, jax.random.fold_in(rng, 6)
    for position, parts in cuts:
        draws = jnp.exp(jax.random.uniform(jax.random.fold_in(own, position), (parts,), jnp.float32, least / len(cuts), top_value / len(cuts)))
        loudness = loudness * jnp.repeat(draws, dims[position] // parts).reshape([-1 if axis == position else 1 for axis in range(len(dims))])
    return loudness


def gaussian(key, extent, deviation, limit, split=(), held_as=jnp.bfloat16):
    loudness = shard_levels(key, extent, split, -0.22, 0.18) if split else 1.0
    values = jax.random.normal(key, extent, jnp.float32) * deviation * loudness
    return jnp.minimum(jnp.maximum(values, -limit), limit).astype(held_as)


def setup_inputs(seed: int = 0) -> dict:
    splits = jax.random.split(jax.random.key(seed), 17)
    inputs = gaussian(splits[0], (MICRO, MBT, D), 1.0, 6.0, ((1, 32),))
    cotangent = draw_cotangent(jax.random.fold_in(splits[16], 71), 0)
    projector = gaussian(splits[2], (D, 3 * D), D ** -0.5, 0.21875, ((0, 8), (1, 4)))
    projector_bias = gaussian(splits[3], (3 * D,), 0.3, 2.0, ((0, 4),))
    combiner = gaussian(splits[4], (D, D), (0.6 * (SEQ / D) ** 0.5), 6.0, ((0, 8), (1, 4)))
    combiner_bias = gaussian(splits[5], (D,), 0.3, 2.0, (), jnp.float32)
    attend_gain = jnp.clip(1.0 + 0.1 * jax.random.normal(splits[6], (D,), jnp.float32), 0.5, 1.5)
    attend_shift = gaussian(splits[7], (D,), 0.3, 2.0, (), jnp.float32)
    expander = gaussian(splits[8], (D, FF), D ** -0.5, 0.21875, ((0, 8), (1, 4)))
    expander_bias = gaussian(splits[9], (FF,), 0.3, 2.0, ((0, 4),))
    reducer = gaussian(splits[10], (FF, D), FF ** -0.5, 0.109375, ((0, 4), (1, 8)))
    reducer_bias = gaussian(splits[11], (D,), 0.3, 2.0, (), jnp.float32)
    final_gain = jnp.clip(1.0 + 0.1 * jax.random.normal(splits[12], (D,), jnp.float32), 0.5, 1.5)
    final_shift = gaussian(splits[13], (D,), 0.3, 2.0, (), jnp.float32)
    projection = gaussian(splits[14], (M, DH), 1.0, 4.0, (), jnp.float32)
    lengths = draw_lengths(jax.random.fold_in(splits[16], 71), 0)
    return dict(inputs=inputs, cotangent=cotangent, projector=projector, projector_bias=projector_bias, combiner=combiner, combiner_bias=combiner_bias, attend_gain=attend_gain, attend_shift=attend_shift, expander=expander, expander_bias=expander_bias, reducer=reducer, reducer_bias=reducer_bias, final_gain=final_gain, final_shift=final_shift, projection=projection, lengths=lengths)


layer_eps = 1e-06
largest_logit = lax.Precision.HIGHEST

@jax.custom_vjp
def low(v):
    return lax.optimization_barrier(v.astype(jnp.bfloat16)).astype(jnp.float32)

@jax.custom_vjp
def low_back(v):
    return v

def low_keep(v):
    return (low(v), None)

def low_pass(kept, grad):
    return (grad,)

def back_keep(v):
    return (v, None)

def back_low(kept, grad):
    return (low(grad),)
low.defvjp(low_keep, low_pass)
low_back.defvjp(back_keep, back_low)

def layer_norm(values, gain_vector, shift_vector):
    midpoint_shift = values - lax.optimization_barrier(jnp.mean(values, axis=-1, keepdims=True))
    spread = lax.optimization_barrier(jnp.mean(midpoint_shift * midpoint_shift, axis=-1, keepdims=True))
    return midpoint_shift * lax.rsqrt(spread + layer_eps) * gain_vector + shift_vector

def feature_map(vectors, omegas):
    scaled = vectors * vectors.shape[-1] ** (-0.25)
    angles = jnp.einsum('thd,md->thm', scaled, omegas, precision=largest_logit)
    energy = 0.5 * lax.optimization_barrier(jnp.sum(scaled * scaled, axis=-1, keepdims=True))
    return jnp.exp(angles - energy) * omegas.shape[0] ** (-0.5)

def micro_forward(token_rows, keep_mask, omegas, projector, projector_bias, combiner, combiner_bias, attend_gain, attend_shift, expander, expander_bias, reducer, reducer_bias, final_gain, final_shift):
    token_count = token_rows.shape[0]
    mixed = jnp.dot(token_rows, projector, precision=largest_logit) + projector_bias
    mixed = low(low_back(mixed))
    query_rows = mixed[:, :D].reshape(token_count, H, DH)
    key_rows = mixed[:, D:2 * D].reshape(token_count, H, DH)
    value_matrix = mixed[:, 2 * D:].reshape(token_count, H, DH)
    query_random_features = feature_map(query_rows, omegas).reshape(MB_SEQS, SEQ, H, M)
    key_random_features = (feature_map(key_rows, omegas) * keep_mask[:, None, None]).reshape(MB_SEQS, SEQ, H, M)
    value_seq = value_matrix.reshape(MB_SEQS, SEQ, H, DH)
    key_value_state = jnp.einsum('sthm,sthd->shmd', key_random_features, value_seq, precision=largest_logit)
    norm_total = lax.optimization_barrier(jnp.sum(key_random_features, axis=1))
    numerator_rows = jnp.einsum('sthm,shmd->sthd', query_random_features, key_value_state, precision=largest_logit)
    denom = jnp.einsum('sthm,shm->sth', query_random_features, norm_total, precision=largest_logit)
    attended = low((numerator_rows / denom[..., None]).reshape(token_count, D))
    branch = low_back(jnp.dot(attended, combiner, precision=largest_logit) + combiner_bias)
    normed = low(layer_norm(token_rows + branch, attend_gain, attend_shift))
    pre_act = low_back(jnp.dot(normed, expander, precision=largest_logit) + expander_bias)
    hidden = low(jax.nn.gelu(pre_act, approximate=False))
    shrunk = low_back(jnp.dot(hidden, reducer, precision=largest_logit) + reducer_bias)
    return layer_norm(normed + shrunk, final_gain, final_shift)

def reference(inputs, cotangent, projector, projector_bias, combiner, combiner_bias, attend_gain, attend_shift, expander, expander_bias, reducer, reducer_bias, final_gain, final_shift, projection, lengths):
    params = tuple((weight_arg.astype(jnp.float32) for weight_arg in (projector, projector_bias, combiner, combiner_bias, attend_gain, attend_shift, expander, expander_bias, reducer, reducer_bias, final_gain, final_shift)))
    omegas = projection.astype(jnp.float32)
    slot_index = jnp.arange(MB_SEQS * SEQ, dtype=jnp.int32)
    outputs = []
    input_grads = []
    totals = tuple((jnp.zeros(weight_arg.shape, jnp.float32) for weight_arg in params))
    for micro_index in range(MICRO):
        bounds = lengths[micro_index * MB_SEQS + slot_index // SEQ]
        keep_mask = (slot_index % SEQ < bounds).astype(jnp.float32)

        def forward_fn(token_rows, *weights):
            return micro_forward(token_rows, keep_mask, omegas, *weights)
        result, pull_back = jax.vjp(forward_fn, inputs[micro_index].astype(jnp.float32), *params)
        gradients = pull_back(cotangent[micro_index].astype(jnp.float32))
        outputs.append(result.astype(jnp.bfloat16))
        input_grads.append(gradients[0])
        totals = tuple((running + update for running, update in zip(totals, gradients[1:])))
    return (jnp.stack(outputs), jnp.stack(input_grads), totals[0], totals[1], totals[2], totals[3], totals[4], totals[5], totals[6], totals[7], totals[8], totals[9], totals[10], totals[11])
```

```python
import jax
import jax.numpy as jnp
from jax import lax
from jax.experimental import pallas as pl
from jax.experimental.pallas import tpu as pltpu
from jax.sharding import PartitionSpec as P

layer_eps = 1e-06
BF = jnp.bfloat16
F32 = jnp.float32
MIB = 1024 * 1024


def nt(left, right):
    return lax.dot_general(left, right, (((1,), (1,)), ((), ())), preferred_element_type=F32)


def tn(left, right):
    return lax.dot_general(left, right, (((0,), (0,)), ((), ())), preferred_element_type=F32)


def nn(left, right):
    return jnp.dot(left, right, preferred_element_type=F32)


def down(values):
    return jnp.sum(values, axis=0, keepdims=True)


def across(values):
    return jnp.sum(values, axis=1, keepdims=True)


def halves(shape):
    return lax.broadcasted_iota(jnp.int32, shape, 1) < shape[1] // 2


def beside(*parts):
    return jnp.concatenate(parts, axis=1)


def lanes_up(n):
    return -(-n // 128) * 128


def project_kernel(xh_ref, xf_ref, pa_ref, pb_ref, bias_ref, here_ref, away_ref):
    pa, pb, bias = pa_ref[0], pb_ref[0], bias_ref[0]
    extra = jnp.zeros((xh_ref.shape[0], bias.shape[1] - pa.shape[1] - pb.shape[1]), F32)
    for x_ref, out_ref in ((xh_ref, here_ref), (xf_ref, away_ref)):
        x = x_ref[...]
        out_ref[0] = (beside(nn(x, pa), nn(x, pb), extra) + bias).astype(BF)


def project_back_kernel(gh_ref, gf_ref, pa_ref, pb_ref, resid_ref, here_ref, away_ref, acc_ref):
    y = pl.program_id(0)
    cut = pa_ref.shape[2]

    @pl.when(y == 0)
    def _():
        here_ref[...] = resid_ref[...]
        acc_ref[...] = jnp.zeros_like(acc_ref)

    pa, pb = pa_ref[0], pb_ref[0]
    gh, gf = gh_ref[0], gf_ref[0]
    end = cut + pb.shape[1]
    here_ref[...] += nt(gh[:, :cut], pa) + nt(gh[:, cut:end], pb)
    acc_ref[...] += nt(gf[:, :cut], pa) + nt(gf[:, cut:end], pb)

    @pl.when(y == pl.num_programs(0) - 1)
    def _():
        away_ref[...] = acc_ref[...].astype(BF)


def pair_features(u, rhs, scale, weight):
    uf = u.astype(F32)
    squares = uf * uf * (0.5 * scale * scale)
    low = halves(squares.shape)
    first = across(jnp.where(low, squares, 0.0))
    second = across(jnp.where(low, 0.0, squares))
    angles = nn(beside(u, u), rhs)
    m = angles.shape[1] // 2
    return beside(jnp.exp(angles[:, :m] - first) * weight, jnp.exp(angles[:, m:] - second) * weight)


def pick(both):
    m = both.shape[0] // 2
    return jnp.where(halves((m, both.shape[1])), both[:m], both[m:])


def put_totals(msg_ref, tot_ref, base):
    msg_ref[base : base + tot_ref.shape[0]] = tot_ref[...].astype(BF)


def row_to_rows(tot_ref, start, row):
    n = tot_ref.shape[1]
    for k in range(row.shape[1] // n):
        tot_ref[start + k : start + k + 1] = row[:, k * n : (k + 1) * n]


def rows_to_row(msg_ref, start, count):
    rows = msg_ref[start : start + count].astype(F32)
    return beside(*[rows[k : k + 1] for k in range(count)])


def features_kernel(
    scale, weight, n_proj, idx_ref, here_ref, far_ref, rhs_ref, keep_ref, mixed_ref, fq_ref, fk_ref, msg_ref, tot_ref
):
    cols2 = here_ref.shape[0]
    lanes = keep_ref.shape[1]
    pairs, _, wide = fq_ref.shape
    feats = wide // 2

    def assemble(even, odd):
        mixed_ref[...] = beside(*[r[y][:, :n_proj] for y in range(cols2) for r in (even, odd)])

    pl.when(idx_ref[0] == 0)(lambda: assemble(here_ref, far_ref))
    pl.when(idx_ref[0] == 1)(lambda: assemble(far_ref, here_ref))
    rhs = rhs_ref[...]
    keep = keep_ref[:, :1]
    tot_ref[...] = jnp.zeros_like(tot_ref)
    per = wide // lanes

    def column(block):
        return mixed_ref[:, block * lanes : (block + 1) * lanes]

    for p in range(pairs):
        fk = (pair_features(column(pairs + p), rhs, scale, weight) * keep).astype(BF)
        fk_ref[p] = fk
        msg_ref[p * feats : (p + 1) * feats] = pick(tn(fk, column(2 * pairs + p))).astype(BF)
        row_to_rows(tot_ref, p * per, down(fk.astype(F32)))
        fq_ref[p] = pair_features(column(p), rhs, scale, weight).astype(BF)
    put_totals(msg_ref, tot_ref, pairs * feats)


def pair_sums(msg_ref, p, pairs, feats, per):
    return msg_ref[p * feats : (p + 1) * feats], rows_to_row(msg_ref, pairs * feats + p * per, per)


def read_pair(fq, st, total):
    feats, lanes = st.shape
    weighted = fq.astype(F32) * total
    low = halves((fq.shape[0], lanes))
    rd = 1.0 / jnp.where(low, across(weighted[:, :feats]), across(weighted[:, feats:]))
    return jnp.where(low, nn(fq[:, :feats], st), nn(fq[:, feats:], st)) * rd, rd


def pull_features(g, u, back, scale):
    both = nn(g, back)
    n = u.shape[1]
    return scale * (both[:, :n] - scale * both[:, n:] * u.astype(F32))


def query_back_pair(scale, da, a, rd, fq, st, total, u, back):
    feats = st.shape[0]
    dnum = (da * rd).astype(BF)
    prod = dnum.astype(F32) * a
    low = halves(prod.shape)
    dden0 = -across(jnp.where(low, prod, 0.0))
    dden1 = -across(jnp.where(low, 0.0, prod))
    none = jnp.zeros_like(dnum)
    fqf = fq.astype(F32)
    f0, f1 = fqf[:, :feats], fqf[:, feats:]
    g0 = (nt(jnp.where(low, dnum, none), st) + dden0 * total[:, :feats]) * f0
    g1 = (nt(jnp.where(low, none, dnum), st) + dden1 * total[:, feats:]) * f1
    dq = pull_features(beside(g0, g1).astype(BF), u, back, scale).astype(BF)
    return dq, pick(tn(fq, dnum)).astype(BF), beside(down(f0 * dden0), down(f1 * dden1))


def key_back_kernel(scale, n, idx_ref, fk_ref, msg_ref, mixed_ref, dq_ref, back_ref, here_ref, away_ref, all_ref):
    pairs, _, wide = fk_ref.shape
    feats, lanes = wide // 2, msg_ref.shape[1]
    per = wide // lanes
    back = back_ref[...]
    all_ref[:, : pairs * lanes] = dq_ref[...]
    for p in range(pairs):
        k_at = slice((pairs + p) * lanes, (pairs + p + 1) * lanes)
        v_at = slice((2 * pairs + p) * lanes, (2 * pairs + p + 1) * lanes)
        fk = fk_ref[p]
        sg = msg_ref[p * feats : (p + 1) * feats]
        tg = rows_to_row(msg_ref, pairs * feats + p * per, per)
        v = mixed_ref[:, v_at]
        low = halves(v.shape)
        zero = jnp.zeros_like(v)
        fkf = fk.astype(F32)
        g0 = (nt(jnp.where(low, v, zero), sg) + tg[:, :feats]) * fkf[:, :feats]
        g1 = (nt(jnp.where(low, zero, v), sg) + tg[:, feats:]) * fkf[:, feats:]
        all_ref[:, k_at] = pull_features(beside(g0, g1).astype(BF), mixed_ref[:, k_at], back, scale).astype(BF)
        all_ref[:, v_at] = jnp.where(low, nn(fk[:, :feats], sg), nn(fk[:, feats:], sg)).astype(BF)
    cols2, tokens, n_pad = here_ref.shape

    def share(even_ref, odd_ref):
        for y in range(cols2):
            for k, ref in ((0, even_ref), (1, odd_ref)):
                c = 2 * y + k
                block = all_ref[:, c * n : (c + 1) * n]
                ref[y] = beside(block, jnp.zeros((tokens, n_pad - n), BF)) if n_pad > n else block

    pl.when(idx_ref[0] == 0)(lambda: share(here_ref, away_ref))
    pl.when(idx_ref[0] == 1)(lambda: share(away_ref, here_ref))


def norm_parts(values):
    centred = values - jnp.mean(values, axis=-1, keepdims=True)
    r = lax.rsqrt(jnp.mean(centred * centred, axis=-1, keepdims=True) + layer_eps)
    return centred * r, r


def norm_pull(dy, vhat, r, gain):
    dg = dy * gain
    return r * (
        dg - jnp.mean(dg, axis=-1, keepdims=True) - vhat * jnp.mean(dg * vhat, axis=-1, keepdims=True)
    )


def middle_kernel(
    scale,
    idx_ref,
    fq_ref,
    msg_ref,
    q_ref,
    back_ref,
    x_ref,
    cot_ref,
    vec_ref,
    eb_ref,
    comb_own_ref,
    comb_far_ref,
    expd_own_ref,
    expd_far_ref,
    redu_own_ref,
    redu_far_ref,
    at_ref,
    out_ref,
    normed_ref,
    hid_here_ref,
    hid_away_ref,
    pre_here_ref,
    pre_away_ref,
    shrink_ref,
    bg_here_ref,
    bg_away_ref,
    resid_ref,
    sums_ref,
    ebg_here_ref,
    ebg_away_ref,
    dq_ref,
    msg_out_ref,
    acc_ref,
    vhat_ref,
    r_ref,
    gf_ref,
    slope_ref,
    a_ref,
    rd_ref,
    tot_ref,
):
    phase, c = pl.program_id(0), pl.program_id(1)
    cols = pl.num_programs(1)
    width = x_ref.shape[1]
    cols2 = hid_here_ref.shape[0]
    step = width // (2 * cols2)
    core = idx_ref[0]
    y, k = lax.div(c, 2), lax.rem(c, 2)
    pairs, _, wide = fq_ref.shape
    feats, lanes = wide // 2, msg_ref.shape[1]
    per = wide // lanes

    def comb(ref, b):
        rows = ref.shape[0] // cols2
        return ref[b * rows : (b + 1) * rows].reshape(width, -1)[:, :step]

    @pl.when((phase == 0) & (c == 0))
    def _():
        for p in range(pairs):
            here = slice(p * lanes, (p + 1) * lanes)
            a, rd = read_pair(fq_ref[p], *pair_sums(msg_ref, p, pairs, feats, per))
            a_ref[:, here] = a
            rd_ref[:, here] = rd
            at_ref[:, here] = a.astype(BF)
        at = at_ref[...]

        def attend(even_ref, odd_ref):
            acc_ref[...] = beside(*[nn(at, comb(ref, b)) for b in range(cols2) for ref in (even_ref, odd_ref)])

        pl.when(core == 0)(lambda: attend(comb_own_ref, comb_far_ref))
        pl.when(core == 1)(lambda: attend(comb_far_ref, comb_own_ref))
        vhat, r = norm_parts(x_ref[...].astype(F32) + (acc_ref[...] + vec_ref[0:1]))
        vhat_ref[...] = vhat
        r_ref[...] = r
        normed_ref[...] = (vhat * vec_ref[1:2] + vec_ref[2:3]).astype(BF)
        acc_ref[...] = jnp.zeros_like(acc_ref)

    def forward(expd_ref, redu_ref, hid_ref):
        pre = nn(normed_ref[...], expd_ref[...].reshape(width, -1)) + eb_ref[0]
        cdf = 0.5 * (1.0 + lax.erf(pre * 0.7071067811865476))
        hidden = (pre * cdf).astype(BF)
        hid_ref[pl.ds(y, 1)] = hidden[None]
        slope = cdf + pre * (jnp.exp(-0.5 * pre * pre) * 0.3989422804014327)
        slope_ref[pl.ds(c, 1)] = slope[None]
        acc_ref[...] += nt(hidden, redu_ref[...].reshape(width, -1))

    pl.when((phase == 0) & (k == 0))(lambda: forward(expd_own_ref, redu_own_ref, hid_here_ref))
    pl.when((phase == 0) & (k == 1))(lambda: forward(expd_far_ref, redu_far_ref, hid_away_ref))

    @pl.when((phase == 0) & (c == cols - 1))
    def _():
        vhat, r = norm_parts(normed_ref[...].astype(F32) + (acc_ref[...] + vec_ref[3:4]))
        out_ref[...] = (vhat * vec_ref[4:5] + vec_ref[5:6]).astype(BF)
        dy = cot_ref[...].astype(F32)
        gf = norm_pull(dy, vhat, r, vec_ref[4:5])
        gf_ref[...] = gf
        sg = gf.astype(BF)
        shrink_ref[...] = sg
        sums_ref[0:1] = down(dy * vhat)
        sums_ref[1:2] = down(dy)
        sums_ref[5:6] = down(sg.astype(F32))
        acc_ref[...] = jnp.zeros_like(acc_ref)

    def backward(expd_ref, redu_ref, pre_ref, ebg_ref):
        hidden_grad = nn(shrink_ref[...], redu_ref[...].reshape(width, -1))
        pre_grad = (hidden_grad * slope_ref[pl.ds(c, 1)][0]).astype(BF)
        pre_ref[pl.ds(y, 1)] = pre_grad[None]
        ebg_ref[pl.ds(y, 1)] = down(pre_grad.astype(F32))[None]
        acc_ref[...] += nt(pre_grad, expd_ref[...].reshape(width, -1))

    pl.when((phase == 1) & (k == 0))(lambda: backward(expd_own_ref, redu_own_ref, pre_here_ref, ebg_here_ref))
    pl.when((phase == 1) & (k == 1))(lambda: backward(expd_far_ref, redu_far_ref, pre_away_ref, ebg_away_ref))

    @pl.when((phase == 1) & (c == cols - 1))
    def _():
        dy = gf_ref[...] + acc_ref[...]
        vhat = vhat_ref[...]
        resid = norm_pull(dy, vhat, r_ref[...], vec_ref[1:2])
        resid_ref[...] = resid
        bg = resid.astype(BF)
        sums_ref[2:3] = down(dy * vhat)
        sums_ref[3:4] = down(dy)
        sums_ref[4:5] = down(bg.astype(F32))

        def share(even_ref, odd_ref):
            for b in range(2 * cols2):
                (even_ref, odd_ref)[b % 2][b // 2] = bg[:, b * step : (b + 1) * step]

        pl.when(core == 0)(lambda: share(bg_here_ref, bg_away_ref))
        pl.when(core == 1)(lambda: share(bg_away_ref, bg_here_ref))
        da = jnp.zeros(acc_ref.shape, F32)
        for b in range(cols2):
            da = da + nt(bg_here_ref[b], comb(comb_own_ref, b)) + nt(bg_away_ref[b], comb(comb_far_ref, b))
        acc_ref[...] = da
        tot_ref[...] = jnp.zeros_like(tot_ref)
        back = back_ref[...]
        for p in range(pairs):
            here = slice(p * lanes, (p + 1) * lanes)
            st, total = pair_sums(msg_ref, p, pairs, feats, per)
            dq, state_grad, total_grad = query_back_pair(
                scale, acc_ref[:, here], a_ref[:, here], rd_ref[:, here], fq_ref[p], st, total, q_ref[:, here], back
            )
            dq_ref[:, here] = dq
            msg_out_ref[p * feats : (p + 1) * feats] = state_grad
            row_to_rows(tot_ref, p * per, total_grad)
        put_totals(msg_out_ref, tot_ref, pairs * feats)


def stacked(values, count):
    return jnp.concatenate([values] * count, axis=0)


def grad_cols_kernel(row_n, idx_ref, lh, lf, rh, rf, *refs):
    *vals, here_ref, away_ref = refs
    k = pl.program_id(0)
    half = pl.num_programs(0)
    for out_ref, bit in ((here_ref, idx_ref[1]), (away_ref, 1 - idx_ref[1])):
        at = pl.ds(bit * half + k, 1)
        grad = tn(lh[...], rh[at][0]) + tn(lf[...], rf[at][0])
        if vals:
            grad = beside(grad, stacked(vals[0][at][0], row_n))
        out_ref[0] = grad.astype(BF)


def grad_rows_kernel(row_n, idx_ref, lh_ref, lf_ref, rh_ref, rf_ref, here_ref, away_ref, scr_ref):
    grad = tn(lh_ref[...], rh_ref[0]) + tn(lf_ref[...], rf_ref[0])
    scr_ref[...] = grad.astype(BF).reshape(scr_ref.shape)
    b = idx_ref[2]
    for z in range(row_n // 2):
        here_ref[0, z] = scr_ref[2 * z + b]
        away_ref[0, z] = scr_ref[2 * z + 1 - b]


def flat_rows(row, lanes, rows):
    count = -(-row.shape[1] // lanes)
    row = beside(row, jnp.zeros((1, count * lanes - row.shape[1]), F32)) if row.shape[1] % lanes else row
    parts = [row[:, k * lanes : (k + 1) * lanes] for k in range(count)]
    return jnp.concatenate(parts + [jnp.zeros((rows - count, lanes), F32)], axis=0)


def grad_project_kernel(row_n, cut, n, idx_ref, lh_ref, lf_ref, rh_ref, rf_ref, ha_ref, aa_ref, hb_ref, ab_ref, scr_ref):
    y = pl.program_id(0)
    half = pl.num_programs(0) // 2
    rh, rf = rh_ref[0], rf_ref[0]
    grad = tn(lh_ref[...], rh) + tn(lf_ref[...], rf)
    first = grad[:, :cut].astype(BF)
    mine = lax.div(y, half) == idx_ref[1]
    k = lax.rem(y, half)

    @pl.when(mine)
    def _():
        ha_ref[pl.ds(k, 1)] = first[None]

    @pl.when(jnp.logical_not(mine))
    def _():
        aa_ref[pl.ds(k, 1)] = first[None]

    _, i_rows, lanes = scr_ref.shape
    bias = (down(rh.astype(F32)) + down(rf.astype(F32)))[:, :n]
    side = stacked(flat_rows(bias, lanes - (n - cut), i_rows), row_n)
    scr_ref[...] = beside(grad[:, cut:n], side).astype(BF).reshape(scr_ref.shape)
    b = idx_ref[2]
    for z in range(row_n // 2):
        hb_ref[0, z] = scr_ref[2 * z + b]
        ab_ref[0, z] = scr_ref[2 * z + 1 - b]


def on_device(
    inputs,
    cotangent,
    projector,
    projector_bias,
    combiner,
    combiner_bias,
    attend_gain,
    attend_shift,
    expander,
    expander_bias,
    reducer,
    reducer_bias,
    final_gain,
    final_shift,
    projection,
    lengths,
):
    row_n, col_n = lax.axis_size("row"), lax.axis_size("col")
    row_i, col_i = lax.axis_index("row"), lax.axis_index("col")
    mesh_axes = ("row", "col")
    micro, tok, width = inputs.shape
    feats, head = projection.shape
    i_rows, n_proj = projector.shape
    n_exp, n_com = expander.shape[1], combiner.shape[1]
    assert lengths.shape[0] == micro and col_n % micro == 0 and width % (2 * head) == 0
    assert col_n & (col_n - 1) == 0 and row_n & (row_n - 1) == 0
    sub = col_n // micro
    pairs = width // (2 * head)
    lanes = 2 * head
    tokens = micro * tok
    cols2 = col_n // 2
    scale = float(head) ** -0.25
    weight = float(feats) ** -0.5
    token_groups = [[g + sub * j for j in range(micro)] for g in range(sub)]
    seq_groups = [[r * col_n + j * sub + g for r in range(row_n) for g in range(sub)] for j in range(micro)]
    seq_n = row_n * sub

    def tie(values, *after):
        return lax.optimization_barrier((values, after))[0]

    def sds(shape, dtype):
        return jax.ShapeDtypeStruct(shape, dtype)

    def whole(array):
        rank = len(array.shape)
        return pl.BlockSpec(array.shape, lambda *g: (0,) * rank)

    def lead(array):
        rank = len(array.shape)
        return pl.BlockSpec((1,) + array.shape[1:], lambda y: (y,) + (0,) * (rank - 1))

    smem = pl.BlockSpec(memory_space=pltpu.SMEM)

    def kernel(name, body, args, outs, grid=(1,), in_specs=None, out_specs=None, scratch=(), vmem=58):
        return pl.pallas_call(
            body,
            grid=grid,
            in_specs=in_specs or [smem if a.dtype == jnp.int32 else whole(a) for a in args],
            out_specs=out_specs or [whole(o) for o in outs],
            out_shape=outs,
            scratch_shapes=list(scratch),
            compiler_params=pltpu.CompilerParams(
                dimension_semantics=("arbitrary",) * len(grid), vmem_limit_bytes=vmem * MIB
            ),
            name=name,
        )(*args)

    def gate(values, after):
        return pl.pallas_call(
            lambda values_ref, after_ref, out_ref: None,
            in_specs=[pl.BlockSpec(memory_space=pl.ANY)] * 2,
            out_specs=pl.BlockSpec(memory_space=pl.ANY),
            out_shape=sds(values.shape, values.dtype),
            input_output_aliases={0: 0},
            name="gate",
        )(values, after)

    def to_seq(blocks):
        return lax.all_to_all(
            blocks, "col", split_axis=0, concat_axis=0, tiled=True, axis_index_groups=token_groups
        )

    def seq_a2a(rows):
        return lax.all_to_all(
            rows, mesh_axes, split_axis=0, concat_axis=0, tiled=True, axis_index_groups=seq_groups
        )

    def flip(values, axis, bit):
        mask = bit * (col_n if axis == "row" else 1)
        return lax.ppermute(values, mesh_axes, [(d, d ^ mask) for d in range(row_n * col_n)])

    def bit_of(axis, bit):
        return (lax.axis_index(axis) // bit) % 2

    col_bits = [("col", 1 << k) for k in reversed(range(1, (col_n - 1).bit_length()))]
    row_bits = [("row", 1 << k) for k in reversed(range((row_n - 1).bit_length()))]
    all_bits = col_bits + row_bits
    order_a = col_bits + row_bits[::-1]
    order_b = row_bits[-1:] + col_bits + row_bits[:-1]
    core_bit = ("col", 1)
    core = bit_of(*core_bit)
    index = jnp.stack([core, bit_of(*col_bits[0]), bit_of(*row_bits[-1])]).astype(jnp.int32)

    def spread(block, order, live=()):
        live = list(live)
        for name in order:
            live = [n for n in all_bits if n in live or n == name]
            d = live.index(name)
            other = flip(block, *name)
            block = jnp.where(
                bit_of(*name) == 0, jnp.stack([block, other], axis=d), jnp.stack([other, block], axis=d)
            )
        return block, live

    def pad_lanes(a, n):
        return jnp.pad(a, ((0, 0), (0, n - a.shape[1])))

    cut = lanes_up(n_proj // 2)
    block, live = spread(projector, row_bits[:-1])
    part_a = spread(block[..., :cut], row_bits[-1:] + col_bits, live)[0].reshape(cols2, width, -1)
    part_b = spread(block[..., cut:], col_bits + row_bits[-1:], live)[0].reshape(cols2, width, -1)
    proj_bias = spread(projector_bias.astype(F32), col_bits)[0].reshape(cols2, 1, -1)
    expd_bias = spread(expander_bias.astype(F32), col_bits)[0].reshape(cols2, 1, -1)
    expd_bias = jnp.stack([expd_bias, flip(expd_bias, *core_bit)], axis=1).reshape(col_n, 1, -1)

    n_expd, n_comb = lanes_up(n_exp), lanes_up(n_com)
    packed = jnp.concatenate(
        [pad_lanes(expander, n_expd), pad_lanes(reducer.T, n_expd), pad_lanes(combiner, n_comb)], axis=1
    )
    core_groups = [[r * col_n + 2 * y + k for y in range(cols2) for r in range(row_n)] for k in range(2)]
    later = lax.all_gather(packed, mesh_axes, axis=0, tiled=True, axis_index_groups=core_groups)
    arrived = to_seq(jnp.concatenate([inputs, cotangent], axis=1))
    x, cot = (a.reshape(tokens, width) for a in (arrived[:, :tok], arrived[:, tok:]))
    x_far = flip(x, *core_bit)
    seq_id = col_i // sub
    slot = (row_i * col_n + col_i % sub + sub * jnp.arange(micro, dtype=jnp.int32))[:, None] * tok + jnp.arange(
        tok, dtype=jnp.int32
    )
    keep = (slot.reshape(tokens, 1) < lengths[seq_id]).astype(F32)
    keep = jnp.broadcast_to(keep, (tokens, lanes))

    omega_t = projection.T * scale
    high = lax.reduce_precision(omega_t, 8, 7)
    rest = (omega_t - high).astype(BF)
    high = high.astype(BF)
    none = jnp.zeros_like(high)
    rhs = jnp.concatenate([beside(high, none), beside(none, high), beside(rest, none), beside(none, rest)], axis=0)
    omega = projection.astype(BF)
    ones = jnp.ones_like(omega)
    blank = jnp.zeros_like(omega)
    back = jnp.concatenate([beside(omega, blank, ones, blank), beside(blank, omega, blank, ones)], axis=0)
    vec = jnp.stack([combiner_bias, attend_gain, attend_shift, reducer_bias, final_gain, final_shift])
    ebias = jnp.pad(expd_bias, ((0, 0), (0, 0), (0, n_expd - n_exp)))

    tw = (tokens, width)
    n_pad = lanes_up(n_proj)
    own = sds((cols2, tokens, n_pad), BF)
    proj_bias = jnp.pad(proj_bias, ((0, 0), (0, 0), (0, n_pad - n_proj)))
    here, away = kernel(
        "project",
        project_kernel,
        (x, x_far, part_a, part_b, proj_bias),
        [own, own],
        grid=(cols2,),
        in_specs=[whole(x), whole(x_far), lead(part_a), lead(part_b), lead(proj_bias)],
        out_specs=[lead(own), lead(own)],
    )
    far = flip(away, *core_bit)

    tot_rows = pairs * 2 * feats // lanes
    tot_rows = -(-tot_rows // 16) * 16
    used = pairs * feats + tot_rows
    msg_rows = -(-used // (16 * seq_n)) * 16 * seq_n
    part_rows = msg_rows // seq_n
    msg_shape = sds((msg_rows, lanes), BF)
    feat_shape = sds((pairs, tokens, 2 * feats), BF)
    tot_scratch = pltpu.VMEM((msg_rows - pairs * feats, lanes), F32)

    def reduce_part(arrived):
        mine = jnp.sum(arrived.reshape(seq_n, part_rows, lanes).astype(F32), axis=0).astype(BF)
        return jnp.tile(mine, (seq_n, 1))

    mixed, fq, fk, msg = kernel(
        "features",
        lambda *refs: features_kernel(scale, weight, n_proj, *refs),
        (index, here, far, rhs, keep),
        [sds((tokens, 3 * width), BF), feat_shape, feat_shape, msg_shape],
        scratch=[tot_scratch],
    )
    parts = reduce_part(seq_a2a(msg))
    state = seq_a2a(parts)
    later = gate(later, parts)
    later_far = flip(later, *core_bit).reshape(cols2 * row_n, i_rows, -1)
    later = later.reshape(cols2 * row_n, i_rows, -1)
    def fixed(shape):
        return pl.BlockSpec(shape, lambda p, c: (0,) * len(shape))

    half_shape = (cols2, tokens, n_expd)
    comb_shape = (cols2, tokens, n_com)
    outs = [
        sds(tw, BF),
        sds(tw, BF),
        sds(tw, BF),
        sds(half_shape, BF),
        sds(half_shape, BF),
        sds(half_shape, BF),
        sds(half_shape, BF),
        sds(tw, BF),
        sds(comb_shape, BF),
        sds(comb_shape, BF),
        sds(tw, F32),
        sds((8, width), F32),
        sds((cols2, 1, n_expd), F32),
        sds((cols2, 1, n_expd), F32),
        sds(tw, BF),
        msg_shape,
    ]

    def weight_spec(n, place):
        return pl.BlockSpec((row_n, i_rows, n), lambda p, c: (c // 2, 0, place))

    comb_spec = pl.BlockSpec((cols2 * row_n, i_rows, n_comb), lambda p, c: (0, 0, 2 * n_expd // n_comb))
    (
        attended,
        layer_out,
        normed,
        hid_here,
        hid_away,
        pre_here,
        pre_away,
        shrink_grad,
        bg_here,
        bg_away,
        resid_grad,
        sums,
        ebg_here,
        ebg_away,
        dq,
        msg,
    ) = kernel(
        "middle",
        lambda *refs: middle_kernel(scale, *refs),
        (index, fq, state, mixed, back, x, cot, vec, ebias) + (later, later_far) * 3,
        outs,
        grid=(2, col_n),
        in_specs=[
            smem,
            fixed(fq.shape),
            fixed(state.shape),
            fixed(tw),
            fixed(back.shape),
            fixed(tw),
            fixed(tw),
            fixed(vec.shape),
            pl.BlockSpec((1, 1, n_expd), lambda p, c: (c, 0, 0)),
            comb_spec,
            comb_spec,
            weight_spec(n_expd, 0),
            weight_spec(n_expd, 0),
            weight_spec(n_expd, 1),
            weight_spec(n_expd, 1),
        ],
        out_specs=[fixed(o.shape) for o in outs],
        scratch=[
            pltpu.VMEM(tw, F32),
            pltpu.VMEM(tw, F32),
            pltpu.VMEM((tokens, 1), F32),
            pltpu.VMEM(tw, F32),
            pltpu.VMEM((col_n, tokens, n_expd), F32),
            pltpu.VMEM(tw, F32),
            pltpu.VMEM(tw, F32),
            tot_scratch,
        ],
        vmem=58,
    )

    arrived = seq_a2a(msg)

    def rounded(a):
        return lax.reduce_precision(a, 8, 7).astype(BF)

    class Stream:
        def __init__(self, order, here, away):
            self.order = list(order)
            self.live = [n for n in all_bits if n != order[0]]
            self.here, self.away = (a.reshape(-1, i_rows, a.shape[-1]) for a in (here, away))

        def send(self):
            self.got = flip(self.away, *self.order.pop(0))

        def hold(self, *after):
            self.got = tie(self.got, *after)

        def split(self):
            name = self.order[0]
            d = self.live.index(name)
            b = bit_of(*name)
            blocks, _, n = self.here.shape
            view = (1 << d, 2, (blocks >> (d + 1)) * i_rows, n)
            here, got = self.here.reshape(view), self.got.reshape(view)

            def side(bit):
                a, g = (lax.dynamic_index_in_dim(v, bit, 1, keepdims=False) for v in (here, got))
                return rounded(a.astype(F32) + g.astype(F32)).reshape(blocks // 2, i_rows, n)

            self.away, self.here = side(1 - b), side(b)
            self.live.remove(name)

        def last(self):
            return (self.here.astype(F32) + self.got.astype(F32)).reshape(i_rows, -1)

    (
        normed,
        shrink_grad,
        attended,
        hid_here,
        hid_away,
        pre_here,
        pre_away,
        bg_here,
        bg_away,
        ebg_here,
        ebg_away,
        sums,
    ) = tie(
        (
            normed,
            shrink_grad,
            attended,
            hid_here,
            hid_away,
            pre_here,
            pre_away,
            bg_here,
            bg_away,
            ebg_here,
            ebg_away,
            sums,
        ),
        msg,
    )
    hid_far, pre_far, bg_far = (flip(a, *core_bit) for a in (hid_away, pre_away, bg_away))
    shrink_far, normed_far, attended_far = (flip(a, *core_bit) for a in (shrink_grad, normed, attended))
    small = jnp.tile(sums[:6].reshape(1, -1), (cols2, 1))
    small_here = beside(ebg_here.reshape(cols2, -1), small)
    small_here = small_here + flip(beside(ebg_away.reshape(cols2, -1), small), *core_bit)
    count = small_here.shape[1]
    extra = lanes_up(n_com + -(-count // i_rows)) - n_com
    small_here = jnp.pad(small_here, ((0, 0), (0, i_rows * extra - count))).reshape(cols2, i_rows, extra)

    row_out = sds((cols2, row_n // 2, i_rows, n_expd), BF)

    def grad_cols(name, left, left_far, right, right_far, *vals):
        out = sds((cols2 // 2, width, right.shape[-1] + sum(v.shape[-1] for v in vals)), BF)
        return kernel(
            name,
            lambda *refs: grad_cols_kernel(row_n, *refs),
            (index, left, left_far, right, right_far) + vals,
            [out, out],
            grid=(cols2 // 2,),
            out_specs=[lead(out), lead(out)],
        )

    expd_s = Stream(
        order_b,
        *kernel(
            "expander_grad",
            lambda *refs: grad_rows_kernel(row_n, *refs),
            (index, normed, normed_far, pre_here, pre_far),
            [row_out, row_out],
            grid=(cols2,),
            in_specs=[smem, whole(normed), whole(normed_far), lead(pre_here), lead(pre_far)],
            out_specs=[lead(row_out), lead(row_out)],
            scratch=[pltpu.VMEM((row_n, i_rows, n_expd), BF)],
        ),
    )
    redu_s = Stream(order_a, *grad_cols("reducer_grad", shrink_grad, shrink_far, hid_here, hid_far))
    comb_s = Stream(order_a, *grad_cols("combiner_grad", attended, attended_far, bg_here, bg_far, small_here))
    expd_s.send()
    redu_s.send()
    comb_s.send()
    parts = reduce_part(tie(arrived, redu_s.away, expd_s.away))
    state_grad = seq_a2a(parts)
    streams = (expd_s, redu_s, comb_s)
    for s in streams:
        s.hold(parts)
        s.split()
        s.send()
    state_grad = tie(state_grad, *[s.away for s in streams])

    grad_here, grad_away = kernel(
        "key_back",
        lambda *refs: key_back_kernel(scale, n_proj, *refs),
        (index, fk, state_grad, mixed, dq, back),
        [own, own],
        scratch=[pltpu.VMEM((tokens, 3 * width), BF)],
    )
    grad_far = flip(grad_away, *core_bit)
    n_side = lanes_up(n_proj - cut + -(-n_proj // i_rows))
    out_a = sds((cols2 // 2, width, cut), BF)
    out_b = sds((cols2, row_n // 2, i_rows, n_side), BF)
    here_a, away_a, here_b, away_b = kernel(
        "projector_grad",
        lambda *refs: grad_project_kernel(row_n, cut, n_proj, *refs),
        (index, x, x_far, grad_here, grad_far),
        [out_a, out_a, out_b, out_b],
        grid=(cols2,),
        in_specs=[smem, whole(x), whole(x_far), lead(grad_here), lead(grad_far)],
        out_specs=[whole(out_a), whole(out_a), lead(out_b), lead(out_b)],
        scratch=[pltpu.VMEM((row_n, i_rows, n_side), BF)],
    )
    proj_s = (Stream(order_a, here_a, away_a), Stream(order_b, here_b, away_b))
    for s in proj_s:
        s.send()

    def advance(group, *after):
        done = list(after)
        for s in group:
            s.hold(*done)
            s.split()
            s.send()
            done = [s.away]
        return done[0]

    last = advance(proj_s, advance(streams, away_a, away_b))
    gh, gf = tie((grad_here, grad_far), last)
    mine, other = kernel(
        "project_back",
        project_back_kernel,
        (gh, gf, part_a, part_b, resid_grad),
        [sds(tw, F32), sds(tw, BF)],
        grid=(cols2,),
        in_specs=[lead(gh), lead(gf), lead(part_a), lead(part_b), whole(resid_grad)],
        scratch=[pltpu.VMEM(tw, F32)],
    )
    other_far = flip(other, *core_bit)
    last = other
    for _ in range(len(all_bits) - 3):
        last = advance(proj_s, advance(streams, last))
    input_grad = (mine + tie(other_far, last).astype(F32)).astype(BF).reshape(micro, tok, width)
    sent = to_seq(jnp.concatenate([layer_out.reshape(micro, tok, width), input_grad], axis=1))
    layer_out, input_grad = sent[:, :tok], sent[:, tok:].astype(F32)
    last = advance(proj_s, last)
    for s in streams:
        s.hold(last)
    expd_grad, redu_grad, comb_grad = (s.last() for s in streams)
    proj_grad = jnp.concatenate([s.last() for s in proj_s], axis=-1)

    pb = proj_grad[:, n_proj:].reshape(-1)[:n_proj]
    small = comb_grad[:, n_com:].reshape(-1)
    vec = [small[n_expd + i * width : n_expd + (i + 1) * width] for i in range(6)]
    return (
        layer_out,
        input_grad,
        proj_grad[:, :n_proj],
        pb,
        comb_grad[:, :n_com],
        vec[4],
        vec[2],
        vec[3],
        expd_grad[:, :n_exp],
        small[:n_exp],
        redu_grad[:, :n_exp].T,
        vec[5],
        vec[0],
        vec[1],
    )


def solution(mesh):
    placed = (
        P(None, ("row", "col"), None),
        P(None, ("row", "col"), None),
        P("row", "col"),
        P("col"),
        P("row", "col"),
        P(),
        P(),
        P(),
        P("row", "col"),
        P("col"),
        P("col", "row"),
        P(),
        P(),
        P(),
        P(),
        P(),
    )
    return jax.shard_map(
        on_device,
        mesh=mesh,
        in_specs=placed,
        out_specs=(
            P(None, ("row", "col"), None),
            P(None, ("row", "col"), None),
            P("row", "col"),
            P("col"),
            P("row", "col"),
            P(),
            P(),
            P(),
            P("row", "col"),
            P("col"),
            P("col", "row"),
            P(),
            P(),
            P(),
        ),
        check_vma=False,
    )
```

```python
import jax
import jax.numpy as jnp
from jax import lax
from jax.experimental import pallas as pl
from jax.experimental.pallas import tpu as pltpu
from jax.sharding import PartitionSpec as P

layer_eps = 1e-06
BF = jnp.bfloat16
F32 = jnp.float32
MIB = 1024 * 1024


def nt(left, right):
    return lax.dot_general(left, right, (((1,), (1,)), ((), ())), preferred_element_type=F32)


def tn(left, right):
    return lax.dot_general(left, right, (((0,), (0,)), ((), ())), preferred_element_type=F32)


def nn(left, right):
    return jnp.dot(left, right, preferred_element_type=F32)


def down(values):
    return jnp.sum(values, axis=0, keepdims=True)


def across(values):
    return jnp.sum(values, axis=1, keepdims=True)


def halves(shape):
    return lax.broadcasted_iota(jnp.int32, shape, 1) < shape[1] // 2


def beside(*parts):
    return jnp.concatenate(parts, axis=1)


def lanes_up(n):
    return -(-n // 128) * 128


def project_kernel(xh_ref, xf_ref, pa_ref, pb_ref, bias_ref, here_ref, away_ref):
    pa, pb, bias = pa_ref[0], pb_ref[0], bias_ref[0]
    extra = jnp.zeros((xh_ref.shape[0], bias.shape[1] - pa.shape[1] - pb.shape[1]), F32)
    for x_ref, out_ref in ((xh_ref, here_ref), (xf_ref, away_ref)):
        x = x_ref[...]
        out_ref[0] = (beside(nn(x, pa), nn(x, pb), extra) + bias).astype(BF)


def project_back_kernel(gh_ref, gf_ref, pa_ref, pb_ref, resid_ref, here_ref, away_ref, acc_ref):
    y = pl.program_id(0)
    cut = pa_ref.shape[2]

    @pl.when(y == 0)
    def _():
        here_ref[...] = resid_ref[...]
        acc_ref[...] = jnp.zeros_like(acc_ref)

    pa, pb = pa_ref[0], pb_ref[0]
    gh, gf = gh_ref[0], gf_ref[0]
    end = cut + pb.shape[1]
    here_ref[...] += nt(gh[:, :cut], pa) + nt(gh[:, cut:end], pb)
    acc_ref[...] += nt(gf[:, :cut], pa) + nt(gf[:, cut:end], pb)

    @pl.when(y == pl.num_programs(0) - 1)
    def _():
        away_ref[...] = acc_ref[...].astype(BF)


def pair_features(u, rhs, scale, weight):
    uf = u.astype(F32)
    squares = uf * uf * (0.5 * scale * scale)
    low = halves(squares.shape)
    first = across(jnp.where(low, squares, 0.0))
    second = across(jnp.where(low, 0.0, squares))
    angles = nn(beside(u, u), rhs)
    m = angles.shape[1] // 2
    return beside(jnp.exp(angles[:, :m] - first) * weight, jnp.exp(angles[:, m:] - second) * weight)


def pick(both):
    m = both.shape[0] // 2
    return jnp.where(halves((m, both.shape[1])), both[:m], both[m:])


def put_totals(msg_ref, tot_ref, base):
    msg_ref[base : base + tot_ref.shape[0]] = tot_ref[...].astype(BF)


def row_to_rows(tot_ref, start, row):
    n = tot_ref.shape[1]
    for k in range(row.shape[1] // n):
        tot_ref[start + k : start + k + 1] = row[:, k * n : (k + 1) * n]


def rows_to_row(msg_ref, start, count):
    rows = msg_ref[start : start + count].astype(F32)
    return beside(*[rows[k : k + 1] for k in range(count)])


def features_kernel(
    scale, weight, n_proj, idx_ref, here_ref, far_ref, rhs_ref, keep_ref, mixed_ref, fq_ref, fk_ref, msg_ref, tot_ref
):
    cols2 = here_ref.shape[0]
    lanes = keep_ref.shape[1]
    pairs, _, wide = fq_ref.shape
    feats = wide // 2

    def assemble(even, odd):
        mixed_ref[...] = beside(*[r[y][:, :n_proj] for y in range(cols2) for r in (even, odd)])

    pl.when(idx_ref[0] == 0)(lambda: assemble(here_ref, far_ref))
    pl.when(idx_ref[0] == 1)(lambda: assemble(far_ref, here_ref))
    rhs = rhs_ref[...]
    keep = keep_ref[:, :1]
    tot_ref[...] = jnp.zeros_like(tot_ref)
    per = wide // lanes

    def column(block):
        return mixed_ref[:, block * lanes : (block + 1) * lanes]

    for p in range(pairs):
        fk = (pair_features(column(pairs + p), rhs, scale, weight) * keep).astype(BF)
        fk_ref[p] = fk
        msg_ref[p * feats : (p + 1) * feats] = pick(tn(fk, column(2 * pairs + p))).astype(BF)
        row_to_rows(tot_ref, p * per, down(fk.astype(F32)))
        fq_ref[p] = pair_features(column(p), rhs, scale, weight).astype(BF)
    put_totals(msg_ref, tot_ref, pairs * feats)


def pair_sums(msg_ref, p, pairs, feats, per):
    return msg_ref[p * feats : (p + 1) * feats], rows_to_row(msg_ref, pairs * feats + p * per, per)


def read_pair(fq, st, total):
    feats, lanes = st.shape
    weighted = fq.astype(F32) * total
    low = halves((fq.shape[0], lanes))
    rd = 1.0 / jnp.where(low, across(weighted[:, :feats]), across(weighted[:, feats:]))
    return jnp.where(low, nn(fq[:, :feats], st), nn(fq[:, feats:], st)) * rd, rd


def pull_features(g, u, back, scale):
    both = nn(g, back)
    n = u.shape[1]
    return scale * (both[:, :n] - scale * both[:, n:] * u.astype(F32))


def query_back_pair(scale, da, a, rd, fq, st, total, u, back):
    feats = st.shape[0]
    dnum = (da * rd).astype(BF)
    prod = dnum.astype(F32) * a
    low = halves(prod.shape)
    dden0 = -across(jnp.where(low, prod, 0.0))
    dden1 = -across(jnp.where(low, 0.0, prod))
    none = jnp.zeros_like(dnum)
    fqf = fq.astype(F32)
    f0, f1 = fqf[:, :feats], fqf[:, feats:]
    g0 = (nt(jnp.where(low, dnum, none), st) + dden0 * total[:, :feats]) * f0
    g1 = (nt(jnp.where(low, none, dnum), st) + dden1 * total[:, feats:]) * f1
    dq = pull_features(beside(g0, g1).astype(BF), u, back, scale).astype(BF)
    return dq, pick(tn(fq, dnum)).astype(BF), beside(down(f0 * dden0), down(f1 * dden1))


def key_back_kernel(scale, n, idx_ref, fk_ref, msg_ref, mixed_ref, dq_ref, back_ref, here_ref, away_ref, all_ref):
    pairs, _, wide = fk_ref.shape
    feats, lanes = wide // 2, msg_ref.shape[1]
    per = wide // lanes
    back = back_ref[...]
    all_ref[:, : pairs * lanes] = dq_ref[...]
    for p in range(pairs):
        k_at = slice((pairs + p) * lanes, (pairs + p + 1) * lanes)
        v_at = slice((2 * pairs + p) * lanes, (2 * pairs + p + 1) * lanes)
        fk = fk_ref[p]
        sg = msg_ref[p * feats : (p + 1) * feats]
        tg = rows_to_row(msg_ref, pairs * feats + p * per, per)
        v = mixed_ref[:, v_at]
        low = halves(v.shape)
        zero = jnp.zeros_like(v)
        fkf = fk.astype(F32)
        g0 = (nt(jnp.where(low, v, zero), sg) + tg[:, :feats]) * fkf[:, :feats]
        g1 = (nt(jnp.where(low, zero, v), sg) + tg[:, feats:]) * fkf[:, feats:]
        all_ref[:, k_at] = pull_features(beside(g0, g1).astype(BF), mixed_ref[:, k_at], back, scale).astype(BF)
        all_ref[:, v_at] = jnp.where(low, nn(fk[:, :feats], sg), nn(fk[:, feats:], sg)).astype(BF)
    cols2, tokens, n_pad = here_ref.shape

    def share(even_ref, odd_ref):
        for y in range(cols2):
            for k, ref in ((0, even_ref), (1, odd_ref)):
                c = 2 * y + k
                block = all_ref[:, c * n : (c + 1) * n]
                ref[y] = beside(block, jnp.zeros((tokens, n_pad - n), BF)) if n_pad > n else block

    pl.when(idx_ref[0] == 0)(lambda: share(here_ref, away_ref))
    pl.when(idx_ref[0] == 1)(lambda: share(away_ref, here_ref))


def norm_parts(values):
    centred = values - jnp.mean(values, axis=-1, keepdims=True)
    r = lax.rsqrt(jnp.mean(centred * centred, axis=-1, keepdims=True) + layer_eps)
    return centred * r, r


def norm_pull(dy, vhat, r, gain):
    dg = dy * gain
    return r * (
        dg - jnp.mean(dg, axis=-1, keepdims=True) - vhat * jnp.mean(dg * vhat, axis=-1, keepdims=True)
    )


def middle_kernel(
    scale,
    idx_ref,
    fq_ref,
    msg_ref,
    q_ref,
    back_ref,
    x_ref,
    cot_ref,
    vec_ref,
    eb_ref,
    comb_own_ref,
    comb_far_ref,
    expd_own_ref,
    expd_far_ref,
    redu_own_ref,
    redu_far_ref,
    at_ref,
    out_ref,
    normed_ref,
    hid_here_ref,
    hid_away_ref,
    pre_here_ref,
    pre_away_ref,
    shrink_ref,
    bg_here_ref,
    bg_away_ref,
    resid_ref,
    sums_ref,
    ebg_here_ref,
    ebg_away_ref,
    dq_ref,
    msg_out_ref,
    acc_ref,
    vhat_ref,
    r_ref,
    gf_ref,
    slope_ref,
    a_ref,
    rd_ref,
    tot_ref,
):
    phase, c = pl.program_id(0), pl.program_id(1)
    cols = pl.num_programs(1)
    width = x_ref.shape[1]
    cols2 = hid_here_ref.shape[0]
    step = width // (2 * cols2)
    core = idx_ref[0]
    y, k = lax.div(c, 2), lax.rem(c, 2)
    pairs, _, wide = fq_ref.shape
    feats, lanes = wide // 2, msg_ref.shape[1]
    per = wide // lanes

    def comb(ref, b):
        rows = ref.shape[0] // cols2
        return ref[b * rows : (b + 1) * rows].reshape(width, -1)[:, :step]

    @pl.when((phase == 0) & (c == 0))
    def _():
        for p in range(pairs):
            here = slice(p * lanes, (p + 1) * lanes)
            a, rd = read_pair(fq_ref[p], *pair_sums(msg_ref, p, pairs, feats, per))
            a_ref[:, here] = a
            rd_ref[:, here] = rd
            at_ref[:, here] = a.astype(BF)
        at = at_ref[...]

        def attend(even_ref, odd_ref):
            acc_ref[...] = beside(*[nn(at, comb(ref, b)) for b in range(cols2) for ref in (even_ref, odd_ref)])

        pl.when(core == 0)(lambda: attend(comb_own_ref, comb_far_ref))
        pl.when(core == 1)(lambda: attend(comb_far_ref, comb_own_ref))
        vhat, r = norm_parts(x_ref[...].astype(F32) + (acc_ref[...] + vec_ref[0:1]))
        vhat_ref[...] = vhat
        r_ref[...] = r
        normed_ref[...] = (vhat * vec_ref[1:2] + vec_ref[2:3]).astype(BF)
        acc_ref[...] = jnp.zeros_like(acc_ref)

    def forward(expd_ref, redu_ref, hid_ref):
        expd, bias, normed = expd_ref[...].reshape(width, -1), eb_ref[0], normed_ref[...]
        n = expd.shape[1]
        wide = 256 if n % 256 == 0 else n
        hidden = []
        for j in range(0, n, wide):
            cols_j = slice(j, j + wide)
            pre = nn(normed, expd[:, cols_j]) + bias[:, cols_j]
            cdf = 0.5 * (1.0 + lax.erf(pre * 0.7071067811865476))
            hidden.append((pre * cdf).astype(BF))
            slope = cdf + pre * (jnp.exp(-0.5 * pre * pre) * 0.3989422804014327)
            slope_ref[pl.ds(c, 1), :, cols_j] = slope[None]
        hidden = beside(*hidden)
        hid_ref[pl.ds(y, 1)] = hidden[None]
        acc_ref[...] += nt(hidden, redu_ref[...].reshape(width, -1))

    pl.when((phase == 0) & (k == 0))(lambda: forward(expd_own_ref, redu_own_ref, hid_here_ref))
    pl.when((phase == 0) & (k == 1))(lambda: forward(expd_far_ref, redu_far_ref, hid_away_ref))

    @pl.when((phase == 0) & (c == cols - 1))
    def _():
        vhat, r = norm_parts(normed_ref[...].astype(F32) + (acc_ref[...] + vec_ref[3:4]))
        out_ref[...] = (vhat * vec_ref[4:5] + vec_ref[5:6]).astype(BF)
        dy = cot_ref[...].astype(F32)
        gf = norm_pull(dy, vhat, r, vec_ref[4:5])
        gf_ref[...] = gf
        sg = gf.astype(BF)
        shrink_ref[...] = sg
        sums_ref[0:1] = down(dy * vhat)
        sums_ref[1:2] = down(dy)
        sums_ref[5:6] = down(sg.astype(F32))
        acc_ref[...] = jnp.zeros_like(acc_ref)

    def backward(expd_ref, redu_ref, pre_ref, ebg_ref):
        hidden_grad = nn(shrink_ref[...], redu_ref[...].reshape(width, -1))
        pre_grad = (hidden_grad * slope_ref[pl.ds(c, 1)][0]).astype(BF)
        pre_ref[pl.ds(y, 1)] = pre_grad[None]
        ebg_ref[pl.ds(y, 1)] = down(pre_grad.astype(F32))[None]
        acc_ref[...] += nt(pre_grad, expd_ref[...].reshape(width, -1))

    pl.when((phase == 1) & (k == 0))(lambda: backward(expd_own_ref, redu_own_ref, pre_here_ref, ebg_here_ref))
    pl.when((phase == 1) & (k == 1))(lambda: backward(expd_far_ref, redu_far_ref, pre_away_ref, ebg_away_ref))

    @pl.when((phase == 1) & (c == cols - 1))
    def _():
        dy = gf_ref[...] + acc_ref[...]
        vhat = vhat_ref[...]
        resid = norm_pull(dy, vhat, r_ref[...], vec_ref[1:2])
        resid_ref[...] = resid
        bg = resid.astype(BF)
        sums_ref[2:3] = down(dy * vhat)
        sums_ref[3:4] = down(dy)
        sums_ref[4:5] = down(bg.astype(F32))

        def share(even_ref, odd_ref):
            for b in range(2 * cols2):
                (even_ref, odd_ref)[b % 2][b // 2] = bg[:, b * step : (b + 1) * step]

        pl.when(core == 0)(lambda: share(bg_here_ref, bg_away_ref))
        pl.when(core == 1)(lambda: share(bg_away_ref, bg_here_ref))
        da = jnp.zeros(acc_ref.shape, F32)
        for b in range(cols2):
            da = da + nt(bg_here_ref[b], comb(comb_own_ref, b)) + nt(bg_away_ref[b], comb(comb_far_ref, b))
        acc_ref[...] = da
        tot_ref[...] = jnp.zeros_like(tot_ref)
        back = back_ref[...]
        for p in range(pairs):
            here = slice(p * lanes, (p + 1) * lanes)
            st, total = pair_sums(msg_ref, p, pairs, feats, per)
            dq, state_grad, total_grad = query_back_pair(
                scale, acc_ref[:, here], a_ref[:, here], rd_ref[:, here], fq_ref[p], st, total, q_ref[:, here], back
            )
            dq_ref[:, here] = dq
            msg_out_ref[p * feats : (p + 1) * feats] = state_grad
            row_to_rows(tot_ref, p * per, total_grad)
        put_totals(msg_out_ref, tot_ref, pairs * feats)


def stacked(values, count):
    return jnp.concatenate([values] * count, axis=0)


def grad_cols_kernel(idx_ref, lh, lf, rh, rf, here_ref, away_ref):
    k = pl.program_id(0)
    half = pl.num_programs(0)
    for out_ref, bit in ((here_ref, idx_ref[1]), (away_ref, 1 - idx_ref[1])):
        at = pl.ds(bit * half + k, 1)
        out_ref[0] = (tn(lh[...], rh[at][0]) + tn(lf[...], rf[at][0])).astype(BF)


def share_rows(scr_ref, place, b, here_ref, away_ref):
    for n in range(scr_ref.shape[0] // 2):
        low = n & ((1 << place) - 1)
        r = ((n - low) << 1) + low
        here_ref[0, n] = scr_ref[r + (b << place)]
        away_ref[0, n] = scr_ref[r + ((1 - b) << place)]


def grad_rows_kernel(place, idx_ref, lh_ref, lf_ref, rh_ref, rf_ref, *refs):
    *vals, here_ref, away_ref, scr_ref = refs
    grad = tn(lh_ref[...], rh_ref[0]) + tn(lf_ref[...], rf_ref[0])
    if vals:
        grad = beside(grad, stacked(vals[0][0], scr_ref.shape[0]))
    scr_ref[...] = grad.astype(BF).reshape(scr_ref.shape)
    share_rows(scr_ref, place, idx_ref[2 + place], here_ref, away_ref)


def flat_rows(row, lanes, rows):
    count = -(-row.shape[1] // lanes)
    row = beside(row, jnp.zeros((1, count * lanes - row.shape[1]), F32)) if row.shape[1] % lanes else row
    parts = [row[:, k * lanes : (k + 1) * lanes] for k in range(count)]
    return jnp.concatenate(parts + [jnp.zeros((rows - count, lanes), F32)], axis=0)


def grad_project_kernel(row_n, cut, n, idx_ref, lh_ref, lf_ref, rh_ref, rf_ref, ha_ref, aa_ref, hb_ref, ab_ref, scr_ref):
    y = pl.program_id(0)
    half = pl.num_programs(0) // 2
    rh, rf = rh_ref[0], rf_ref[0]
    grad = tn(lh_ref[...], rh) + tn(lf_ref[...], rf)
    first = grad[:, :cut].astype(BF)
    mine = lax.div(y, half) == idx_ref[1]
    k = lax.rem(y, half)

    @pl.when(mine)
    def _():
        ha_ref[pl.ds(k, 1)] = first[None]

    @pl.when(jnp.logical_not(mine))
    def _():
        aa_ref[pl.ds(k, 1)] = first[None]

    _, i_rows, lanes = scr_ref.shape
    bias = (down(rh.astype(F32)) + down(rf.astype(F32)))[:, :n]
    side = stacked(flat_rows(bias, lanes - (n - cut), i_rows), row_n)
    scr_ref[...] = beside(grad[:, cut:n], side).astype(BF).reshape(scr_ref.shape)
    share_rows(scr_ref, 0, idx_ref[2], hb_ref, ab_ref)


def row_of(values, first, count):
    rows = [values[first + k : first + k + 1] for k in range(-(-count // values.shape[1]))]
    return beside(*rows)[:, :count]


def finish_kernel(firsts, here_ref, got_ref, grad_ref, *vec_refs):
    total = here_ref[0].astype(F32) + got_ref[0].astype(F32)
    n = grad_ref.shape[1]
    grad_ref[...] = total[:, :n]
    side = total[:, n:]
    for first, ref in zip(firsts, vec_refs):
        ref[...] = row_of(side, first, ref.shape[0])[0]


def on_device(
    inputs,
    cotangent,
    projector,
    projector_bias,
    combiner,
    combiner_bias,
    attend_gain,
    attend_shift,
    expander,
    expander_bias,
    reducer,
    reducer_bias,
    final_gain,
    final_shift,
    projection,
    lengths,
):
    row_n, col_n = lax.axis_size("row"), lax.axis_size("col")
    row_i, col_i = lax.axis_index("row"), lax.axis_index("col")
    mesh_axes = ("row", "col")
    micro, tok, width = inputs.shape
    feats, head = projection.shape
    i_rows, n_proj = projector.shape
    n_exp, n_com = expander.shape[1], combiner.shape[1]
    assert lengths.shape[0] == micro and col_n % micro == 0 and width % (2 * head) == 0
    assert col_n & (col_n - 1) == 0 and row_n & (row_n - 1) == 0
    sub = col_n // micro
    pairs = width // (2 * head)
    lanes = 2 * head
    tokens = micro * tok
    cols2 = col_n // 2
    scale = float(head) ** -0.25
    weight = float(feats) ** -0.5
    token_groups = [[g + sub * j for j in range(micro)] for g in range(sub)]
    seq_groups = [[r * col_n + j * sub + g for r in range(row_n) for g in range(sub)] for j in range(micro)]
    seq_n = row_n * sub

    def tie(values, *after):
        return lax.optimization_barrier((values, after))[0]

    def sds(shape, dtype):
        return jax.ShapeDtypeStruct(shape, dtype)

    def whole(array):
        rank = len(array.shape)
        return pl.BlockSpec(array.shape, lambda *g: (0,) * rank)

    def lead(array):
        rank = len(array.shape)
        return pl.BlockSpec((1,) + array.shape[1:], lambda y: (y,) + (0,) * (rank - 1))

    smem = pl.BlockSpec(memory_space=pltpu.SMEM)

    def kernel(name, body, args, outs, grid=(1,), in_specs=None, out_specs=None, scratch=(), vmem=58):
        return pl.pallas_call(
            body,
            grid=grid,
            in_specs=in_specs or [smem if a.dtype == jnp.int32 else whole(a) for a in args],
            out_specs=out_specs or [whole(o) for o in outs],
            out_shape=outs,
            scratch_shapes=list(scratch),
            compiler_params=pltpu.CompilerParams(
                dimension_semantics=("arbitrary",) * len(grid), vmem_limit_bytes=vmem * MIB
            ),
            name=name,
        )(*args)

    def gate(values, after):
        return pl.pallas_call(
            lambda values_ref, after_ref, out_ref: None,
            in_specs=[pl.BlockSpec(memory_space=pl.ANY)] * 2,
            out_specs=pl.BlockSpec(memory_space=pl.ANY),
            out_shape=sds(values.shape, values.dtype),
            input_output_aliases={0: 0},
            name="gate",
        )(values, after)

    def to_seq(blocks):
        return lax.all_to_all(
            blocks, "col", split_axis=0, concat_axis=0, tiled=True, axis_index_groups=token_groups
        )

    def seq_a2a(rows):
        return lax.all_to_all(
            rows, mesh_axes, split_axis=0, concat_axis=0, tiled=True, axis_index_groups=seq_groups
        )

    def flip(values, axis, bit):
        mask = bit * (col_n if axis == "row" else 1)
        return lax.ppermute(values, mesh_axes, [(d, d ^ mask) for d in range(row_n * col_n)])

    def bit_of(axis, bit):
        return (lax.axis_index(axis) // bit) % 2

    col_bits = [("col", 1 << k) for k in reversed(range(1, (col_n - 1).bit_length()))]
    row_bits = [("row", 1 << k) for k in reversed(range((row_n - 1).bit_length()))]
    all_bits = col_bits + row_bits
    order_a = col_bits + row_bits[::-1]
    order_b = row_bits[-1:] + col_bits + row_bits[:-1]
    core_bit = ("col", 1)
    core = bit_of(*core_bit)
    order_z = row_bits[:-1][::-1] + row_bits[-1:] + col_bits
    order_x = row_bits[-1:] + row_bits[:-1][::-1] + col_bits
    index = jnp.stack([core, bit_of(*col_bits[0])] + [bit_of(*n) for n in row_bits[::-1]]).astype(jnp.int32)

    def spread(block, order, live=()):
        live = list(live)
        for name in order:
            live = [n for n in all_bits if n in live or n == name]
            d = live.index(name)
            other = flip(block, *name)
            block = jnp.where(
                bit_of(*name) == 0, jnp.stack([block, other], axis=d), jnp.stack([other, block], axis=d)
            )
        return block, live

    def pad_lanes(a, n):
        return jnp.pad(a, ((0, 0), (0, n - a.shape[1])))

    cut = lanes_up(n_proj // 2)
    block, live = spread(projector, row_bits[:-1])
    part_a = spread(block[..., :cut], row_bits[-1:] + col_bits, live)[0].reshape(cols2, width, -1)
    part_b = spread(block[..., cut:], col_bits + row_bits[-1:], live)[0].reshape(cols2, width, -1)
    proj_bias = spread(projector_bias.astype(F32), col_bits)[0].reshape(cols2, 1, -1)
    expd_bias = spread(expander_bias.astype(F32), col_bits)[0].reshape(cols2, 1, -1)
    expd_bias = jnp.stack([expd_bias, flip(expd_bias, *core_bit)], axis=1).reshape(col_n, 1, -1)

    n_expd, n_comb = lanes_up(n_exp), lanes_up(n_com)
    packed = jnp.concatenate(
        [pad_lanes(expander, n_expd), pad_lanes(reducer.T, n_expd), pad_lanes(combiner, n_comb)], axis=1
    )
    core_groups = [[r * col_n + 2 * y + k for y in range(cols2) for r in range(row_n)] for k in range(2)]
    later = lax.all_gather(packed, mesh_axes, axis=0, tiled=True, axis_index_groups=core_groups)
    arrived = to_seq(jnp.concatenate([inputs, cotangent], axis=1))
    x, cot = (a.reshape(tokens, width) for a in (arrived[:, :tok], arrived[:, tok:]))
    x_far = flip(x, *core_bit)
    seq_id = col_i // sub
    slot = (row_i * col_n + col_i % sub + sub * jnp.arange(micro, dtype=jnp.int32))[:, None] * tok + jnp.arange(
        tok, dtype=jnp.int32
    )
    keep = (slot.reshape(tokens, 1) < lengths[seq_id]).astype(F32)
    keep = jnp.broadcast_to(keep, (tokens, lanes))

    omega_t = projection.T * scale
    high = lax.reduce_precision(omega_t, 8, 7)
    rest = (omega_t - high).astype(BF)
    high = high.astype(BF)
    none = jnp.zeros_like(high)
    rhs = jnp.concatenate([beside(high, none), beside(none, high), beside(rest, none), beside(none, rest)], axis=0)
    omega = projection.astype(BF)
    ones = jnp.ones_like(omega)
    blank = jnp.zeros_like(omega)
    back = jnp.concatenate([beside(omega, blank, ones, blank), beside(blank, omega, blank, ones)], axis=0)
    vec = jnp.stack([combiner_bias, attend_gain, attend_shift, reducer_bias, final_gain, final_shift])
    ebias = jnp.pad(expd_bias, ((0, 0), (0, 0), (0, n_expd - n_exp)))

    tw = (tokens, width)
    n_pad = lanes_up(n_proj)
    own = sds((cols2, tokens, n_pad), BF)
    proj_bias = jnp.pad(proj_bias, ((0, 0), (0, 0), (0, n_pad - n_proj)))
    here, away = kernel(
        "project",
        project_kernel,
        (x, x_far, part_a, part_b, proj_bias),
        [own, own],
        grid=(cols2,),
        in_specs=[whole(x), whole(x_far), lead(part_a), lead(part_b), lead(proj_bias)],
        out_specs=[lead(own), lead(own)],
    )
    far = flip(away, *core_bit)

    tot_rows = pairs * 2 * feats // lanes
    tot_rows = -(-tot_rows // 16) * 16
    used = pairs * feats + tot_rows
    msg_rows = -(-used // (16 * seq_n)) * 16 * seq_n
    part_rows = msg_rows // seq_n
    msg_shape = sds((msg_rows, lanes), BF)
    feat_shape = sds((pairs, tokens, 2 * feats), BF)
    tot_scratch = pltpu.VMEM((msg_rows - pairs * feats, lanes), F32)

    def reduce_part(arrived):
        mine = jnp.sum(arrived.reshape(seq_n, part_rows, lanes).astype(F32), axis=0).astype(BF)
        return jnp.tile(mine, (seq_n, 1))

    mixed, fq, fk, msg = kernel(
        "features",
        lambda *refs: features_kernel(scale, weight, n_proj, *refs),
        (index, here, far, rhs, keep),
        [sds((tokens, 3 * width), BF), feat_shape, feat_shape, msg_shape],
        scratch=[tot_scratch],
    )
    parts = reduce_part(seq_a2a(msg))
    state = seq_a2a(parts)
    later = gate(later, parts)
    later_far = flip(later, *core_bit).reshape(cols2 * row_n, i_rows, -1)
    later = later.reshape(cols2 * row_n, i_rows, -1)
    def fixed(shape):
        return pl.BlockSpec(shape, lambda p, c: (0,) * len(shape))

    half_shape = (cols2, tokens, n_expd)
    comb_shape = (cols2, tokens, n_com)
    outs = [
        sds(tw, BF),
        sds(tw, BF),
        sds(tw, BF),
        sds(half_shape, BF),
        sds(half_shape, BF),
        sds(half_shape, BF),
        sds(half_shape, BF),
        sds(tw, BF),
        sds(comb_shape, BF),
        sds(comb_shape, BF),
        sds(tw, F32),
        sds((8, width), F32),
        sds((cols2, 1, n_expd), F32),
        sds((cols2, 1, n_expd), F32),
        sds(tw, BF),
        msg_shape,
    ]

    def weight_spec(n, place):
        return pl.BlockSpec((row_n, i_rows, n), lambda p, c: (c // 2, 0, place))

    comb_spec = pl.BlockSpec((cols2 * row_n, i_rows, n_comb), lambda p, c: (0, 0, 2 * n_expd // n_comb))
    (
        attended,
        layer_out,
        normed,
        hid_here,
        hid_away,
        pre_here,
        pre_away,
        shrink_grad,
        bg_here,
        bg_away,
        resid_grad,
        sums,
        ebg_here,
        ebg_away,
        dq,
        msg,
    ) = kernel(
        "middle",
        lambda *refs: middle_kernel(scale, *refs),
        (index, fq, state, mixed, back, x, cot, vec, ebias) + (later, later_far) * 3,
        outs,
        grid=(2, col_n),
        in_specs=[
            smem,
            fixed(fq.shape),
            fixed(state.shape),
            fixed(tw),
            fixed(back.shape),
            fixed(tw),
            fixed(tw),
            fixed(vec.shape),
            pl.BlockSpec((1, 1, n_expd), lambda p, c: (c, 0, 0)),
            comb_spec,
            comb_spec,
            weight_spec(n_expd, 0),
            weight_spec(n_expd, 0),
            weight_spec(n_expd, 1),
            weight_spec(n_expd, 1),
        ],
        out_specs=[fixed(o.shape) for o in outs],
        scratch=[
            pltpu.VMEM(tw, F32),
            pltpu.VMEM(tw, F32),
            pltpu.VMEM((tokens, 1), F32),
            pltpu.VMEM(tw, F32),
            pltpu.VMEM((col_n, tokens, n_expd), F32),
            pltpu.VMEM(tw, F32),
            pltpu.VMEM(tw, F32),
            tot_scratch,
        ],
        vmem=58,
    )

    arrived = seq_a2a(msg)

    def rounded(a):
        return lax.reduce_precision(a, 8, 7).astype(BF)

    class Stream:
        def __init__(self, order, here, away):
            self.order = list(order)
            self.live = [n for n in all_bits if n != order[0]]
            self.here, self.away = (a.reshape(-1, i_rows, a.shape[-1]) for a in (here, away))

        def send(self):
            self.got = flip(self.away, *self.order.pop(0))

        def hold(self, *after):
            self.got = tie(self.got, *after)

        def split(self):
            name = self.order[0]
            d = self.live.index(name)
            b = bit_of(*name)
            blocks, _, n = self.here.shape
            view = (1 << d, 2, (blocks >> (d + 1)) * i_rows, n)
            here, got = self.here.reshape(view), self.got.reshape(view)

            def side(bit):
                a, g = (lax.dynamic_index_in_dim(v, bit, 1, keepdims=False) for v in (here, got))
                return rounded(a.astype(F32) + g.astype(F32)).reshape(blocks // 2, i_rows, n)

            self.away, self.here = side(1 - b), side(b)
            self.live.remove(name)

        def last(self):
            return (self.here.astype(F32) + self.got.astype(F32)).reshape(i_rows, -1)

    (
        normed,
        shrink_grad,
        attended,
        hid_here,
        hid_away,
        pre_here,
        pre_away,
        bg_here,
        bg_away,
        ebg_here,
        ebg_away,
        sums,
    ) = tie(
        (
            normed,
            shrink_grad,
            attended,
            hid_here,
            hid_away,
            pre_here,
            pre_away,
            bg_here,
            bg_away,
            ebg_here,
            ebg_away,
            sums,
        ),
        msg,
    )
    hid_far, pre_far, bg_far = (flip(a, *core_bit) for a in (hid_away, pre_away, bg_away))
    shrink_far, normed_far, attended_far = (flip(a, *core_bit) for a in (shrink_grad, normed, attended))
    small = jnp.tile(sums[:6].reshape(1, -1), (cols2, 1))
    small_here = beside(ebg_here.reshape(cols2, -1), small)
    small_here = small_here + flip(beside(ebg_away.reshape(cols2, -1), small), *core_bit)
    count = small_here.shape[1]
    extra = lanes_up(n_com + -(-count // i_rows)) - n_com
    small_here = jnp.pad(small_here, ((0, 0), (0, i_rows * extra - count))).reshape(cols2, i_rows, extra)

    def grad_cols(name, left, left_far, right, right_far):
        out = sds((cols2 // 2, width, right.shape[-1]), BF)
        return kernel(
            name,
            grad_cols_kernel,
            (index, left, left_far, right, right_far),
            [out, out],
            grid=(cols2 // 2,),
            out_specs=[lead(out), lead(out)],
        )

    def grad_rows(name, place, left, left_far, right, right_far, *vals):
        n = right.shape[-1] + sum(v.shape[-1] for v in vals)
        out = sds((cols2, row_n // 2, i_rows, n), BF)
        return kernel(
            name,
            lambda *refs: grad_rows_kernel(place, *refs),
            (index, left, left_far, right, right_far) + vals,
            [out, out],
            grid=(cols2,),
            in_specs=[smem, whole(left), whole(left_far)] + [lead(a) for a in (right, right_far) + vals],
            out_specs=[lead(out), lead(out)],
            scratch=[pltpu.VMEM((row_n, i_rows, n), BF)],
        )

    expd_s = Stream(order_x, *grad_rows("expander_grad", 0, normed, normed_far, pre_here, pre_far))
    redu_s = Stream(order_a, *grad_cols("reducer_grad", shrink_grad, shrink_far, hid_here, hid_far))
    comb_s = Stream(
        order_z, *grad_rows("combiner_grad", 1, attended, attended_far, bg_here, bg_far, small_here)
    )
    expd_s.send()
    redu_s.send()
    comb_s.send()
    parts = reduce_part(tie(arrived, redu_s.away, expd_s.away))
    state_grad = seq_a2a(parts)
    streams = (expd_s, redu_s, comb_s)
    for s in streams:
        s.hold(parts)
        s.split()
        s.send()
    state_grad = tie(state_grad, *[s.away for s in streams])

    grad_here, grad_away = kernel(
        "key_back",
        lambda *refs: key_back_kernel(scale, n_proj, *refs),
        (index, fk, state_grad, mixed, dq, back),
        [own, own],
        scratch=[pltpu.VMEM((tokens, 3 * width), BF)],
    )
    grad_far = flip(grad_away, *core_bit)
    n_side = lanes_up(n_proj - cut + -(-n_proj // i_rows))
    out_a = sds((cols2 // 2, width, cut), BF)
    out_b = sds((cols2, row_n // 2, i_rows, n_side), BF)
    here_a, away_a, here_b, away_b = kernel(
        "projector_grad",
        lambda *refs: grad_project_kernel(row_n, cut, n_proj, *refs),
        (index, x, x_far, grad_here, grad_far),
        [out_a, out_a, out_b, out_b],
        grid=(cols2,),
        in_specs=[smem, whole(x), whole(x_far), lead(grad_here), lead(grad_far)],
        out_specs=[whole(out_a), whole(out_a), lead(out_b), lead(out_b)],
        scratch=[pltpu.VMEM((row_n, i_rows, n_side), BF)],
    )
    proj_s = (Stream(order_a, here_a, away_a), Stream(order_b, here_b, away_b))
    for s in proj_s:
        s.send()

    def advance(group, *after):
        done = list(after)
        for s in group:
            s.hold(*done)
            s.split()
            s.send()
            done = [s.away]
        return done[0]

    last = advance(proj_s, advance((expd_s, redu_s), away_a, away_b))
    last = advance((comb_s,), last)
    gh, gf = tie((grad_here, grad_far), last)
    mine, other = kernel(
        "project_back",
        project_back_kernel,
        (gh, gf, part_a, part_b, resid_grad),
        [sds(tw, F32), sds(tw, BF)],
        grid=(cols2,),
        in_specs=[lead(gh), lead(gf), lead(part_a), lead(part_b), whole(resid_grad)],
        scratch=[pltpu.VMEM(tw, F32)],
    )
    other_far = flip(other, *core_bit)
    last = other
    for _ in range(len(all_bits) - 3):
        last = advance(proj_s, advance((expd_s, redu_s), last))
        last = advance((comb_s,), last)
    input_grad = (mine + tie(other_far, last).astype(F32)).astype(BF).reshape(micro, tok, width)
    sent = to_seq(jnp.concatenate([layer_out.reshape(micro, tok, width), input_grad], axis=1))
    layer_out, input_grad = sent[:, :tok], sent[:, tok:].astype(F32)
    last = advance(proj_s, last)
    for s in streams:
        s.hold(last)
    expd_grad, redu_grad = expd_s.last(), redu_s.last()
    proj_grad = jnp.concatenate([s.last() for s in proj_s], axis=-1)
    pb = proj_grad[:, n_proj:].reshape(-1)[:n_proj]
    side = comb_s.here.shape[-1] - n_com
    places = [0] + [n_expd + v * width for v in range(6)]
    if all(place % side == 0 for place in places):
        comb_grad, eb, *vec = kernel(
            "finish",
            lambda *refs: finish_kernel([place // side for place in places], *refs),
            (comb_s.here, comb_s.got),
            [sds((i_rows, n_com), F32), sds((n_exp,), F32)] + [sds((width,), F32)] * 6,
        )
    else:
        comb_grad = comb_s.last()
        small = comb_grad[:, n_com:].reshape(-1)
        comb_grad, eb = comb_grad[:, :n_com], small[:n_exp]
        vec = [small[place : place + width] for place in places[1:]]
    return (
        layer_out,
        input_grad,
        proj_grad[:, :n_proj],
        pb,
        comb_grad,
        vec[4],
        vec[2],
        vec[3],
        expd_grad[:, :n_exp],
        eb,
        redu_grad[:, :n_exp].T,
        vec[5],
        vec[0],
        vec[1],
    )


def solution(mesh):
    placed = (
        P(None, ("row", "col"), None),
        P(None, ("row", "col"), None),
        P("row", "col"),
        P("col"),
        P("row", "col"),
        P(),
        P(),
        P(),
        P("row", "col"),
        P("col"),
        P("col", "row"),
        P(),
        P(),
        P(),
        P(),
        P(),
    )
    return jax.shard_map(
        on_device,
        mesh=mesh,
        in_specs=placed,
        out_specs=(
            P(None, ("row", "col"), None),
            P(None, ("row", "col"), None),
            P("row", "col"),
            P("col"),
            P("row", "col"),
            P(),
            P(),
            P(),
            P("row", "col"),
            P("col"),
            P("col", "row"),
            P(),
            P(),
            P(),
        ),
        check_vma=False,
    )
```

```python
import jax
import jax.numpy as jnp
from jax import lax
from jax.experimental import pallas as pl
from jax.experimental.pallas import tpu as pltpu
from jax.sharding import PartitionSpec as P

layer_eps = 1e-06
BF = jnp.bfloat16
F32 = jnp.float32
MIB = 1024 * 1024


def nt(left, right):
    return lax.dot_general(left, right, (((1,), (1,)), ((), ())), preferred_element_type=F32)


def tn(left, right):
    return lax.dot_general(left, right, (((0,), (0,)), ((), ())), preferred_element_type=F32)


def nn(left, right):
    return jnp.dot(left, right, preferred_element_type=F32)


def down(values):
    return jnp.sum(values, axis=0, keepdims=True)


def across(values):
    return jnp.sum(values, axis=1, keepdims=True)


def halves(shape):
    return lax.broadcasted_iota(jnp.int32, shape, 1) < shape[1] // 2


def beside(*parts):
    return jnp.concatenate(parts, axis=1)


def lanes_up(n):
    return -(-n // 128) * 128


def project_kernel(xh_ref, xf_ref, pa_ref, pb_ref, bias_ref, here_ref, away_ref):
    pa, pb, bias = pa_ref[0], pb_ref[0], bias_ref[0]
    extra = jnp.zeros((xh_ref.shape[0], bias.shape[1] - pa.shape[1] - pb.shape[1]), F32)
    for x_ref, out_ref in ((xh_ref, here_ref), (xf_ref, away_ref)):
        x = x_ref[...]
        out_ref[0] = (beside(nn(x, pa), nn(x, pb), extra) + bias).astype(BF)


def project_back_kernel(gh_ref, gf_ref, pa_ref, pb_ref, resid_ref, here_ref, away_ref, acc_ref):
    y = pl.program_id(0)
    cut = pa_ref.shape[2]

    @pl.when(y == 0)
    def _():
        here_ref[...] = resid_ref[...]
        acc_ref[...] = jnp.zeros_like(acc_ref)

    pa, pb = pa_ref[0], pb_ref[0]
    gh, gf = gh_ref[0], gf_ref[0]
    end = cut + pb.shape[1]
    here_ref[...] += nt(gh[:, :cut], pa) + nt(gh[:, cut:end], pb)
    acc_ref[...] += nt(gf[:, :cut], pa) + nt(gf[:, cut:end], pb)

    @pl.when(y == pl.num_programs(0) - 1)
    def _():
        away_ref[...] = acc_ref[...].astype(BF)


def pair_features(u, rhs, scale, weight):
    uf = u.astype(F32)
    squares = uf * uf * (0.5 * scale * scale)
    low = halves(squares.shape)
    first = across(jnp.where(low, squares, 0.0))
    second = across(jnp.where(low, 0.0, squares))
    angles = nn(beside(u, u), rhs)
    m = angles.shape[1] // 2
    return beside(jnp.exp(angles[:, :m] - first) * weight, jnp.exp(angles[:, m:] - second) * weight)


def pick(both):
    m = both.shape[0] // 2
    return jnp.where(halves((m, both.shape[1])), both[:m], both[m:])


def put_totals(msg_ref, tot_ref, base):
    msg_ref[base : base + tot_ref.shape[0]] = tot_ref[...].astype(BF)


def row_to_rows(tot_ref, start, row):
    n = tot_ref.shape[1]
    for k in range(row.shape[1] // n):
        tot_ref[start + k : start + k + 1] = row[:, k * n : (k + 1) * n]


def rows_to_row(msg_ref, start, count):
    rows = msg_ref[start : start + count].astype(F32)
    return beside(*[rows[k : k + 1] for k in range(count)])


def features_kernel(
    scale, weight, n_proj, idx_ref, here_ref, far_ref, rhs_ref, keep_ref, mixed_ref, fq_ref, fk_ref, msg_ref, tot_ref
):
    cols2 = here_ref.shape[0]
    lanes = keep_ref.shape[1]
    pairs, _, wide = fq_ref.shape
    feats = wide // 2

    def assemble(even, odd):
        mixed_ref[...] = beside(*[r[y][:, :n_proj] for y in range(cols2) for r in (even, odd)])

    pl.when(idx_ref[0] == 0)(lambda: assemble(here_ref, far_ref))
    pl.when(idx_ref[0] == 1)(lambda: assemble(far_ref, here_ref))
    rhs = rhs_ref[...]
    keep = keep_ref[:, :1]
    tot_ref[...] = jnp.zeros_like(tot_ref)
    per = wide // lanes

    def column(block):
        return mixed_ref[:, block * lanes : (block + 1) * lanes]

    for p in range(pairs):
        fk = (pair_features(column(pairs + p), rhs, scale, weight) * keep).astype(BF)
        fk_ref[p] = fk
        msg_ref[p * feats : (p + 1) * feats] = pick(tn(fk, column(2 * pairs + p))).astype(BF)
        row_to_rows(tot_ref, p * per, down(fk.astype(F32)))
        fq_ref[p] = pair_features(column(p), rhs, scale, weight).astype(BF)
    put_totals(msg_ref, tot_ref, pairs * feats)


def pair_sums(msg_ref, p, pairs, feats, per):
    return msg_ref[p * feats : (p + 1) * feats], rows_to_row(msg_ref, pairs * feats + p * per, per)


def read_pair(fq, st, total):
    feats, lanes = st.shape
    weighted = fq.astype(F32) * total
    low = halves((fq.shape[0], lanes))
    rd = 1.0 / jnp.where(low, across(weighted[:, :feats]), across(weighted[:, feats:]))
    return jnp.where(low, nn(fq[:, :feats], st), nn(fq[:, feats:], st)) * rd, rd


def pull_features(g, u, back, scale):
    both = nn(g, back)
    n = u.shape[1]
    return scale * (both[:, :n] - scale * both[:, n:] * u.astype(F32))


def query_back_pair(scale, da, a, rd, fq, st, total, u, back):
    feats = st.shape[0]
    dnum = (da * rd).astype(BF)
    prod = dnum.astype(F32) * a
    low = halves(prod.shape)
    dden0 = -across(jnp.where(low, prod, 0.0))
    dden1 = -across(jnp.where(low, 0.0, prod))
    none = jnp.zeros_like(dnum)
    fqf = fq.astype(F32)
    f0, f1 = fqf[:, :feats], fqf[:, feats:]
    g0 = (nt(jnp.where(low, dnum, none), st) + dden0 * total[:, :feats]) * f0
    g1 = (nt(jnp.where(low, none, dnum), st) + dden1 * total[:, feats:]) * f1
    dq = pull_features(beside(g0, g1).astype(BF), u, back, scale).astype(BF)
    return dq, pick(tn(fq, dnum)).astype(BF), beside(down(f0 * dden0), down(f1 * dden1))


def key_back_kernel(scale, n, idx_ref, fk_ref, msg_ref, mixed_ref, dq_ref, back_ref, here_ref, away_ref, all_ref):
    pairs, _, wide = fk_ref.shape
    feats, lanes = wide // 2, msg_ref.shape[1]
    per = wide // lanes
    back = back_ref[...]
    all_ref[:, : pairs * lanes] = dq_ref[...]
    for p in range(pairs):
        k_at = slice((pairs + p) * lanes, (pairs + p + 1) * lanes)
        v_at = slice((2 * pairs + p) * lanes, (2 * pairs + p + 1) * lanes)
        fk = fk_ref[p]
        sg = msg_ref[p * feats : (p + 1) * feats]
        tg = rows_to_row(msg_ref, pairs * feats + p * per, per)
        v = mixed_ref[:, v_at]
        low = halves(v.shape)
        zero = jnp.zeros_like(v)
        fkf = fk.astype(F32)
        g0 = (nt(jnp.where(low, v, zero), sg) + tg[:, :feats]) * fkf[:, :feats]
        g1 = (nt(jnp.where(low, zero, v), sg) + tg[:, feats:]) * fkf[:, feats:]
        all_ref[:, k_at] = pull_features(beside(g0, g1).astype(BF), mixed_ref[:, k_at], back, scale).astype(BF)
        all_ref[:, v_at] = jnp.where(low, nn(fk[:, :feats], sg), nn(fk[:, feats:], sg)).astype(BF)
    cols2, tokens, n_pad = here_ref.shape

    def share(even_ref, odd_ref):
        for y in range(cols2):
            for k, ref in ((0, even_ref), (1, odd_ref)):
                c = 2 * y + k
                block = all_ref[:, c * n : (c + 1) * n]
                ref[y] = beside(block, jnp.zeros((tokens, n_pad - n), BF)) if n_pad > n else block

    pl.when(idx_ref[0] == 0)(lambda: share(here_ref, away_ref))
    pl.when(idx_ref[0] == 1)(lambda: share(away_ref, here_ref))


def norm_parts(values):
    centred = values - jnp.mean(values, axis=-1, keepdims=True)
    r = lax.rsqrt(jnp.mean(centred * centred, axis=-1, keepdims=True) + layer_eps)
    return centred * r, r


def norm_pull(dy, vhat, r, gain):
    dg = dy * gain
    return r * (
        dg - jnp.mean(dg, axis=-1, keepdims=True) - vhat * jnp.mean(dg * vhat, axis=-1, keepdims=True)
    )


def middle_kernel(
    scale,
    idx_ref,
    fq_ref,
    msg_ref,
    q_ref,
    back_ref,
    x_ref,
    cot_ref,
    vec_ref,
    eb_ref,
    comb_ref,
    expd_own_ref,
    expd_far_ref,
    redu_own_ref,
    redu_far_ref,
    at_ref,
    out_ref,
    normed_ref,
    hid_here_ref,
    hid_away_ref,
    pre_here_ref,
    pre_away_ref,
    shrink_ref,
    bg_here_ref,
    bg_away_ref,
    resid_ref,
    sums_ref,
    ebg_here_ref,
    ebg_away_ref,
    dq_ref,
    msg_out_ref,
    acc_ref,
    vhat_ref,
    r_ref,
    gf_ref,
    slope_ref,
    a_ref,
    rd_ref,
    tot_ref,
):
    phase, c = pl.program_id(0), pl.program_id(1)
    cols = pl.num_programs(1)
    width = x_ref.shape[1]
    cols2 = hid_here_ref.shape[0]
    step = width // (2 * cols2)
    core = idx_ref[0]
    y, k = lax.div(c, 2), lax.rem(c, 2)
    pairs, _, wide = fq_ref.shape
    feats, lanes = wide // 2, msg_ref.shape[1]
    per = wide // lanes

    def comb(far, b):
        rows = comb_ref.shape[0] // (2 * cols2)
        block = 2 * b + (1 - core if far else core)
        return comb_ref[pl.ds(block * rows, rows)].reshape(width, -1)[:, :step]

    @pl.when((phase == 0) & (c == 0))
    def _():
        for p in range(pairs):
            here = slice(p * lanes, (p + 1) * lanes)
            a, rd = read_pair(fq_ref[p], *pair_sums(msg_ref, p, pairs, feats, per))
            a_ref[:, here] = a
            rd_ref[:, here] = rd
            at_ref[:, here] = a.astype(BF)
        at = at_ref[...]

        def attend(even_ref, odd_ref):
            acc_ref[...] = beside(*[nn(at, comb(ref, b)) for b in range(cols2) for ref in (even_ref, odd_ref)])

        pl.when(core == 0)(lambda: attend(False, True))
        pl.when(core == 1)(lambda: attend(True, False))
        vhat, r = norm_parts(x_ref[...].astype(F32) + (acc_ref[...] + vec_ref[0:1]))
        vhat_ref[...] = vhat
        r_ref[...] = r
        normed_ref[...] = (vhat * vec_ref[1:2] + vec_ref[2:3]).astype(BF)
        acc_ref[...] = jnp.zeros_like(acc_ref)

    def forward(expd_ref, redu_ref, hid_ref):
        expd, bias, normed = expd_ref[...].reshape(width, -1), eb_ref[0], normed_ref[...]
        n = expd.shape[1]
        wide = 256 if n % 256 == 0 else n
        hidden = []
        for j in range(0, n, wide):
            cols_j = slice(j, j + wide)
            pre = nn(normed, expd[:, cols_j]) + bias[:, cols_j]
            cdf = 0.5 * (1.0 + lax.erf(pre * 0.7071067811865476))
            hidden.append((pre * cdf).astype(BF))
            slope = cdf + pre * (jnp.exp(-0.5 * pre * pre) * 0.3989422804014327)
            slope_ref[pl.ds(c, 1), :, cols_j] = slope[None]
        hidden = beside(*hidden)
        hid_ref[pl.ds(y, 1)] = hidden[None]
        acc_ref[...] += nt(hidden, redu_ref[...].reshape(width, -1))

    pl.when((phase == 0) & (k == 0))(lambda: forward(expd_own_ref, redu_own_ref, hid_here_ref))
    pl.when((phase == 0) & (k == 1))(lambda: forward(expd_far_ref, redu_far_ref, hid_away_ref))

    @pl.when((phase == 0) & (c == cols - 1))
    def _():
        vhat, r = norm_parts(normed_ref[...].astype(F32) + (acc_ref[...] + vec_ref[3:4]))
        out_ref[...] = (vhat * vec_ref[4:5] + vec_ref[5:6]).astype(BF)
        dy = cot_ref[...].astype(F32)
        gf = norm_pull(dy, vhat, r, vec_ref[4:5])
        gf_ref[...] = gf
        sg = gf.astype(BF)
        shrink_ref[...] = sg
        sums_ref[0:1] = down(dy * vhat)
        sums_ref[1:2] = down(dy)
        sums_ref[5:6] = down(sg.astype(F32))
        acc_ref[...] = jnp.zeros_like(acc_ref)

    def backward(expd_ref, redu_ref, pre_ref, ebg_ref):
        hidden_grad = nn(shrink_ref[...], redu_ref[...].reshape(width, -1))
        pre_grad = (hidden_grad * slope_ref[pl.ds(c, 1)][0]).astype(BF)
        pre_ref[pl.ds(y, 1)] = pre_grad[None]
        ebg_ref[pl.ds(y, 1)] = down(pre_grad.astype(F32))[None]
        acc_ref[...] += nt(pre_grad, expd_ref[...].reshape(width, -1))

    pl.when((phase == 1) & (k == 0))(lambda: backward(expd_own_ref, redu_own_ref, pre_here_ref, ebg_here_ref))
    pl.when((phase == 1) & (k == 1))(lambda: backward(expd_far_ref, redu_far_ref, pre_away_ref, ebg_away_ref))

    @pl.when((phase == 1) & (c == cols - 1))
    def _():
        dy = gf_ref[...] + acc_ref[...]
        vhat = vhat_ref[...]
        resid = norm_pull(dy, vhat, r_ref[...], vec_ref[1:2])
        resid_ref[...] = resid
        bg = resid.astype(BF)
        sums_ref[2:3] = down(dy * vhat)
        sums_ref[3:4] = down(dy)
        sums_ref[4:5] = down(bg.astype(F32))

        def share(even_ref, odd_ref):
            for b in range(2 * cols2):
                (even_ref, odd_ref)[b % 2][b // 2] = bg[:, b * step : (b + 1) * step]

        pl.when(core == 0)(lambda: share(bg_here_ref, bg_away_ref))
        pl.when(core == 1)(lambda: share(bg_away_ref, bg_here_ref))
        da = jnp.zeros(acc_ref.shape, F32)
        for b in range(cols2):
            da = da + nt(bg_here_ref[b], comb(False, b)) + nt(bg_away_ref[b], comb(True, b))
        acc_ref[...] = da
        tot_ref[...] = jnp.zeros_like(tot_ref)
        back = back_ref[...]
        for p in range(pairs):
            here = slice(p * lanes, (p + 1) * lanes)
            st, total = pair_sums(msg_ref, p, pairs, feats, per)
            dq, state_grad, total_grad = query_back_pair(
                scale, acc_ref[:, here], a_ref[:, here], rd_ref[:, here], fq_ref[p], st, total, q_ref[:, here], back
            )
            dq_ref[:, here] = dq
            msg_out_ref[p * feats : (p + 1) * feats] = state_grad
            row_to_rows(tot_ref, p * per, total_grad)
        put_totals(msg_out_ref, tot_ref, pairs * feats)


def stacked(values, count):
    return jnp.concatenate([values] * count, axis=0)


def grad_cols_kernel(idx_ref, lh, lf, rh, rf, here_ref, away_ref):
    k = pl.program_id(0)
    half = pl.num_programs(0)
    for out_ref, bit in ((here_ref, idx_ref[1]), (away_ref, 1 - idx_ref[1])):
        at = pl.ds(bit * half + k, 1)
        out_ref[0] = (tn(lh[...], rh[at][0]) + tn(lf[...], rf[at][0])).astype(BF)


def share_rows(scr_ref, place, b, here_ref, away_ref):
    for n in range(scr_ref.shape[0] // 2):
        low = n & ((1 << place) - 1)
        r = ((n - low) << 1) + low
        here_ref[0, n] = scr_ref[r + (b << place)]
        away_ref[0, n] = scr_ref[r + ((1 - b) << place)]


def grad_rows_kernel(place, idx_ref, lh_ref, lf_ref, rh_ref, rf_ref, *refs):
    *vals, here_ref, away_ref, scr_ref = refs
    grad = tn(lh_ref[...], rh_ref[0]) + tn(lf_ref[...], rf_ref[0])
    if vals:
        grad = beside(grad, stacked(vals[0][0], scr_ref.shape[0]))
    scr_ref[...] = grad.astype(BF).reshape(scr_ref.shape)
    share_rows(scr_ref, place, idx_ref[2 + place], here_ref, away_ref)


def flat_rows(row, lanes, rows):
    count = -(-row.shape[1] // lanes)
    row = beside(row, jnp.zeros((1, count * lanes - row.shape[1]), F32)) if row.shape[1] % lanes else row
    parts = [row[:, k * lanes : (k + 1) * lanes] for k in range(count)]
    return jnp.concatenate(parts + [jnp.zeros((rows - count, lanes), F32)], axis=0)


def grad_project_kernel(row_n, cut, n, idx_ref, lh_ref, lf_ref, rh_ref, rf_ref, ha_ref, aa_ref, hb_ref, ab_ref, scr_ref):
    y = pl.program_id(0)
    half = pl.num_programs(0) // 2
    rh, rf = rh_ref[0], rf_ref[0]
    grad = tn(lh_ref[...], rh) + tn(lf_ref[...], rf)
    first = grad[:, :cut].astype(BF)
    mine = lax.div(y, half) == idx_ref[1]
    k = lax.rem(y, half)

    @pl.when(mine)
    def _():
        ha_ref[pl.ds(k, 1)] = first[None]

    @pl.when(jnp.logical_not(mine))
    def _():
        aa_ref[pl.ds(k, 1)] = first[None]

    _, i_rows, lanes = scr_ref.shape
    bias = (down(rh.astype(F32)) + down(rf.astype(F32)))[:, :n]
    side = stacked(flat_rows(bias, lanes - (n - cut), i_rows), row_n)
    scr_ref[...] = beside(grad[:, cut:n], side).astype(BF).reshape(scr_ref.shape)
    share_rows(scr_ref, 0, idx_ref[2], hb_ref, ab_ref)


def row_of(values, first, count):
    rows = [values[first + k : first + k + 1] for k in range(-(-count // values.shape[1]))]
    return beside(*rows)[:, :count]


def finish_kernel(firsts, here_ref, got_ref, grad_ref, *vec_refs):
    total = here_ref[0].astype(F32) + got_ref[0].astype(F32)
    n = grad_ref.shape[1]
    grad_ref[...] = total[:, :n]
    side = total[:, n:]
    for first, ref in zip(firsts, vec_refs):
        ref[...] = row_of(side, first, ref.shape[0])[0]


def on_device(
    inputs,
    cotangent,
    projector,
    projector_bias,
    combiner,
    combiner_bias,
    attend_gain,
    attend_shift,
    expander,
    expander_bias,
    reducer,
    reducer_bias,
    final_gain,
    final_shift,
    projection,
    lengths,
):
    row_n, col_n = lax.axis_size("row"), lax.axis_size("col")
    row_i, col_i = lax.axis_index("row"), lax.axis_index("col")
    mesh_axes = ("row", "col")
    micro, tok, width = inputs.shape
    feats, head = projection.shape
    i_rows, n_proj = projector.shape
    n_exp, n_com = expander.shape[1], combiner.shape[1]
    assert lengths.shape[0] == micro and col_n % micro == 0 and width % (2 * head) == 0
    assert col_n & (col_n - 1) == 0 and row_n & (row_n - 1) == 0
    sub = col_n // micro
    pairs = width // (2 * head)
    lanes = 2 * head
    tokens = micro * tok
    cols2 = col_n // 2
    scale = float(head) ** -0.25
    weight = float(feats) ** -0.5
    token_groups = [[g + sub * j for j in range(micro)] for g in range(sub)]
    seq_groups = [[r * col_n + j * sub + g for r in range(row_n) for g in range(sub)] for j in range(micro)]
    seq_n = row_n * sub

    def tie(values, *after):
        return lax.optimization_barrier((values, after))[0]

    def sds(shape, dtype):
        return jax.ShapeDtypeStruct(shape, dtype)

    def whole(array):
        rank = len(array.shape)
        return pl.BlockSpec(array.shape, lambda *g: (0,) * rank)

    def lead(array):
        rank = len(array.shape)
        return pl.BlockSpec((1,) + array.shape[1:], lambda y: (y,) + (0,) * (rank - 1))

    smem = pl.BlockSpec(memory_space=pltpu.SMEM)

    def kernel(name, body, args, outs, grid=(1,), in_specs=None, out_specs=None, scratch=(), vmem=58):
        return pl.pallas_call(
            body,
            grid=grid,
            in_specs=in_specs or [smem if a.dtype == jnp.int32 else whole(a) for a in args],
            out_specs=out_specs or [whole(o) for o in outs],
            out_shape=outs,
            scratch_shapes=list(scratch),
            compiler_params=pltpu.CompilerParams(
                dimension_semantics=("arbitrary",) * len(grid), vmem_limit_bytes=vmem * MIB
            ),
            name=name,
        )(*args)

    def gate(values, after):
        return pl.pallas_call(
            lambda values_ref, after_ref, out_ref: None,
            in_specs=[pl.BlockSpec(memory_space=pl.ANY)] * 2,
            out_specs=pl.BlockSpec(memory_space=pl.ANY),
            out_shape=sds(values.shape, values.dtype),
            input_output_aliases={0: 0},
            name="gate",
        )(values, after)

    def to_seq(blocks):
        return lax.all_to_all(
            blocks, "col", split_axis=0, concat_axis=0, tiled=True, axis_index_groups=token_groups
        )

    def seq_a2a(rows):
        return lax.all_to_all(
            rows, mesh_axes, split_axis=0, concat_axis=0, tiled=True, axis_index_groups=seq_groups
        )

    def flip(values, axis, bit):
        mask = bit * (col_n if axis == "row" else 1)
        return lax.ppermute(values, mesh_axes, [(d, d ^ mask) for d in range(row_n * col_n)])

    def bit_of(axis, bit):
        return (lax.axis_index(axis) // bit) % 2

    col_bits = [("col", 1 << k) for k in reversed(range(1, (col_n - 1).bit_length()))]
    row_bits = [("row", 1 << k) for k in reversed(range((row_n - 1).bit_length()))]
    all_bits = col_bits + row_bits
    order_a = col_bits + row_bits[::-1]
    order_b = row_bits[-1:] + col_bits + row_bits[:-1]
    core_bit = ("col", 1)
    core = bit_of(*core_bit)
    order_z = row_bits[:-1][::-1] + row_bits[-1:] + col_bits
    order_x = row_bits[-1:] + row_bits[:-1][::-1] + col_bits
    index = jnp.stack([core, bit_of(*col_bits[0])] + [bit_of(*n) for n in row_bits[::-1]]).astype(jnp.int32)

    def spread(block, order, live=()):
        live = list(live)
        for name in order:
            live = [n for n in all_bits if n in live or n == name]
            d = live.index(name)
            other = flip(block, *name)
            block = jnp.where(
                bit_of(*name) == 0, jnp.stack([block, other], axis=d), jnp.stack([other, block], axis=d)
            )
        return block, live

    def pad_lanes(a, n):
        return jnp.pad(a, ((0, 0), (0, n - a.shape[1])))

    cut = lanes_up(n_proj // 2)
    block, live = spread(projector, row_bits[:-1])
    part_a = spread(block[..., :cut], row_bits[-1:] + col_bits, live)[0].reshape(cols2, width, -1)
    part_b = spread(block[..., cut:], col_bits + row_bits[-1:], live)[0].reshape(cols2, width, -1)
    proj_bias = spread(projector_bias.astype(F32), col_bits)[0].reshape(cols2, 1, -1)
    expd_bias = spread(expander_bias.astype(F32), col_bits)[0].reshape(cols2, 1, -1)
    expd_bias = jnp.stack([expd_bias, flip(expd_bias, *core_bit)], axis=1).reshape(col_n, 1, -1)

    n_expd, n_comb = lanes_up(n_exp), lanes_up(n_com)
    packed = jnp.concatenate(
        [pad_lanes(expander, n_expd), pad_lanes(reducer.T, n_expd), pad_lanes(combiner, n_comb)], axis=1
    )
    later = lax.all_gather(packed, ("col", "row"), axis=0, tiled=True).reshape(col_n * row_n, i_rows, -1)

    arrived = to_seq(jnp.concatenate([inputs, cotangent], axis=1))
    x, cot = (a.reshape(tokens, width) for a in (arrived[:, :tok], arrived[:, tok:]))
    x_far = flip(x, *core_bit)
    seq_id = col_i // sub
    slot = (row_i * col_n + col_i % sub + sub * jnp.arange(micro, dtype=jnp.int32))[:, None] * tok + jnp.arange(
        tok, dtype=jnp.int32
    )
    keep = (slot.reshape(tokens, 1) < lengths[seq_id]).astype(F32)
    keep = jnp.broadcast_to(keep, (tokens, lanes))

    omega_t = projection.T * scale
    high = lax.reduce_precision(omega_t, 8, 7)
    rest = (omega_t - high).astype(BF)
    high = high.astype(BF)
    none = jnp.zeros_like(high)
    rhs = jnp.concatenate([beside(high, none), beside(none, high), beside(rest, none), beside(none, rest)], axis=0)
    omega = projection.astype(BF)
    ones = jnp.ones_like(omega)
    blank = jnp.zeros_like(omega)
    back = jnp.concatenate([beside(omega, blank, ones, blank), beside(blank, omega, blank, ones)], axis=0)
    vec = jnp.stack([combiner_bias, attend_gain, attend_shift, reducer_bias, final_gain, final_shift])
    ebias = jnp.pad(expd_bias, ((0, 0), (0, 0), (0, n_expd - n_exp)))

    tw = (tokens, width)
    n_pad = lanes_up(n_proj)
    own = sds((cols2, tokens, n_pad), BF)
    proj_bias = jnp.pad(proj_bias, ((0, 0), (0, 0), (0, n_pad - n_proj)))
    here, away = kernel(
        "project",
        project_kernel,
        (x, x_far, part_a, part_b, proj_bias),
        [own, own],
        grid=(cols2,),
        in_specs=[whole(x), whole(x_far), lead(part_a), lead(part_b), lead(proj_bias)],
        out_specs=[lead(own), lead(own)],
    )
    far = flip(away, *core_bit)

    tot_rows = pairs * 2 * feats // lanes
    tot_rows = -(-tot_rows // 16) * 16
    used = pairs * feats + tot_rows
    msg_rows = -(-used // (16 * seq_n)) * 16 * seq_n
    part_rows = msg_rows // seq_n
    msg_shape = sds((msg_rows, lanes), BF)
    feat_shape = sds((pairs, tokens, 2 * feats), BF)
    tot_scratch = pltpu.VMEM((msg_rows - pairs * feats, lanes), F32)

    def reduce_part(arrived):
        mine = jnp.sum(arrived.reshape(seq_n, part_rows, lanes).astype(F32), axis=0).astype(BF)
        return jnp.tile(mine, (seq_n, 1))

    mixed, fq, fk, msg = kernel(
        "features",
        lambda *refs: features_kernel(scale, weight, n_proj, *refs),
        (index, here, far, rhs, keep),
        [sds((tokens, 3 * width), BF), feat_shape, feat_shape, msg_shape],
        scratch=[tot_scratch],
    )
    parts = reduce_part(seq_a2a(msg))
    state = seq_a2a(parts)
    def fixed(shape):
        return pl.BlockSpec(shape, lambda p, c, i: (0,) * len(shape))

    half_shape = (cols2, tokens, n_expd)
    comb_shape = (cols2, tokens, n_com)
    outs = [
        sds(tw, BF),
        sds(tw, BF),
        sds(tw, BF),
        sds(half_shape, BF),
        sds(half_shape, BF),
        sds(half_shape, BF),
        sds(half_shape, BF),
        sds(tw, BF),
        sds(comb_shape, BF),
        sds(comb_shape, BF),
        sds(tw, F32),
        sds((8, width), F32),
        sds((cols2, 1, n_expd), F32),
        sds((cols2, 1, n_expd), F32),
        sds(tw, BF),
        msg_shape,
    ]

    def weight_spec(far, place):
        return pl.BlockSpec(
            (row_n, i_rows, n_expd), lambda p, c, i: (c // 2 * 2 + (1 - i[0] if far else i[0]), 0, place)
        )

    comb_spec = pl.BlockSpec((col_n * row_n, i_rows, n_comb), lambda p, c, i: (0, 0, 2 * n_expd // n_comb))
    (
        attended,
        layer_out,
        normed,
        hid_here,
        hid_away,
        pre_here,
        pre_away,
        shrink_grad,
        bg_here,
        bg_away,
        resid_grad,
        sums,
        ebg_here,
        ebg_away,
        dq,
        msg,
    ) = pl.pallas_call(
        lambda *refs: middle_kernel(scale, *refs),
        grid_spec=pltpu.PrefetchScalarGridSpec(
            num_scalar_prefetch=1,
            grid=(2, col_n),
            in_specs=[
                fixed(fq.shape),
                fixed(state.shape),
                fixed(tw),
                fixed(back.shape),
                fixed(tw),
                fixed(tw),
                fixed(vec.shape),
                pl.BlockSpec((1, 1, n_expd), lambda p, c, i: (c, 0, 0)),
                comb_spec,
                weight_spec(False, 0),
                weight_spec(True, 0),
                weight_spec(False, 1),
                weight_spec(True, 1),
            ],
            out_specs=[fixed(o.shape) for o in outs],
            scratch_shapes=[
                pltpu.VMEM(tw, F32),
                pltpu.VMEM(tw, F32),
                pltpu.VMEM((tokens, 1), F32),
                pltpu.VMEM(tw, F32),
                pltpu.VMEM((col_n, tokens, n_expd), F32),
                pltpu.VMEM(tw, F32),
                pltpu.VMEM(tw, F32),
                tot_scratch,
            ],
        ),
        out_shape=outs,
        compiler_params=pltpu.CompilerParams(
            dimension_semantics=("arbitrary", "arbitrary"), vmem_limit_bytes=58 * MIB
        ),
        name="middle",
    )(index, fq, state, mixed, back, x, cot, vec, ebias, later, later, later, later, later)

    arrived = seq_a2a(msg)

    def rounded(a):
        return lax.reduce_precision(a, 8, 7).astype(BF)

    class Stream:
        def __init__(self, order, here, away):
            self.order = list(order)
            self.live = [n for n in all_bits if n != order[0]]
            self.here, self.away = (a.reshape(-1, i_rows, a.shape[-1]) for a in (here, away))

        def send(self):
            self.got = flip(self.away, *self.order.pop(0))

        def hold(self, *after):
            self.got = tie(self.got, *after)

        def split(self):
            name = self.order[0]
            d = self.live.index(name)
            b = bit_of(*name)
            blocks, _, n = self.here.shape
            view = (1 << d, 2, (blocks >> (d + 1)) * i_rows, n)
            here, got = self.here.reshape(view), self.got.reshape(view)

            def side(bit):
                a, g = (lax.dynamic_index_in_dim(v, bit, 1, keepdims=False) for v in (here, got))
                return rounded(a.astype(F32) + g.astype(F32)).reshape(blocks // 2, i_rows, n)

            self.away, self.here = side(1 - b), side(b)
            self.live.remove(name)

        def last(self):
            return (self.here.astype(F32) + self.got.astype(F32)).reshape(i_rows, -1)

    (
        normed,
        shrink_grad,
        attended,
        hid_here,
        hid_away,
        pre_here,
        pre_away,
        bg_here,
        bg_away,
        ebg_here,
        ebg_away,
        sums,
    ) = tie(
        (
            normed,
            shrink_grad,
            attended,
            hid_here,
            hid_away,
            pre_here,
            pre_away,
            bg_here,
            bg_away,
            ebg_here,
            ebg_away,
            sums,
        ),
        msg,
    )
    hid_far, pre_far, bg_far = (flip(a, *core_bit) for a in (hid_away, pre_away, bg_away))
    shrink_far, normed_far, attended_far = (flip(a, *core_bit) for a in (shrink_grad, normed, attended))
    small = jnp.tile(sums[:6].reshape(1, -1), (cols2, 1))
    small_here = beside(ebg_here.reshape(cols2, -1), small)
    small_here = small_here + flip(beside(ebg_away.reshape(cols2, -1), small), *core_bit)
    count = small_here.shape[1]
    extra = lanes_up(n_com + -(-count // i_rows)) - n_com
    small_here = jnp.pad(small_here, ((0, 0), (0, i_rows * extra - count))).reshape(cols2, i_rows, extra)

    def grad_cols(name, left, left_far, right, right_far):
        out = sds((cols2 // 2, width, right.shape[-1]), BF)
        return kernel(
            name,
            grad_cols_kernel,
            (index, left, left_far, right, right_far),
            [out, out],
            grid=(cols2 // 2,),
            out_specs=[lead(out), lead(out)],
        )

    def grad_rows(name, place, left, left_far, right, right_far, *vals):
        n = right.shape[-1] + sum(v.shape[-1] for v in vals)
        out = sds((cols2, row_n // 2, i_rows, n), BF)
        return kernel(
            name,
            lambda *refs: grad_rows_kernel(place, *refs),
            (index, left, left_far, right, right_far) + vals,
            [out, out],
            grid=(cols2,),
            in_specs=[smem, whole(left), whole(left_far)] + [lead(a) for a in (right, right_far) + vals],
            out_specs=[lead(out), lead(out)],
            scratch=[pltpu.VMEM((row_n, i_rows, n), BF)],
        )

    expd_s = Stream(order_x, *grad_rows("expander_grad", 0, normed, normed_far, pre_here, pre_far))
    redu_s = Stream(order_a, *grad_cols("reducer_grad", shrink_grad, shrink_far, hid_here, hid_far))
    comb_s = Stream(
        order_z, *grad_rows("combiner_grad", 1, attended, attended_far, bg_here, bg_far, small_here)
    )
    expd_s.send()
    redu_s.send()
    comb_s.send()
    parts = reduce_part(tie(arrived, redu_s.away, expd_s.away))
    state_grad = seq_a2a(parts)
    streams = (expd_s, redu_s, comb_s)
    for s in streams:
        s.hold(parts)
        s.split()
        s.send()
    state_grad = tie(state_grad, *[s.away for s in streams])

    grad_here, grad_away = kernel(
        "key_back",
        lambda *refs: key_back_kernel(scale, n_proj, *refs),
        (index, fk, state_grad, mixed, dq, back),
        [own, own],
        scratch=[pltpu.VMEM((tokens, 3 * width), BF)],
    )
    grad_far = flip(grad_away, *core_bit)
    n_side = lanes_up(n_proj - cut + -(-n_proj // i_rows))
    out_a = sds((cols2 // 2, width, cut), BF)
    out_b = sds((cols2, row_n // 2, i_rows, n_side), BF)
    here_a, away_a, here_b, away_b = kernel(
        "projector_grad",
        lambda *refs: grad_project_kernel(row_n, cut, n_proj, *refs),
        (index, x, x_far, grad_here, grad_far),
        [out_a, out_a, out_b, out_b],
        grid=(cols2,),
        in_specs=[smem, whole(x), whole(x_far), lead(grad_here), lead(grad_far)],
        out_specs=[whole(out_a), whole(out_a), lead(out_b), lead(out_b)],
        scratch=[pltpu.VMEM((row_n, i_rows, n_side), BF)],
    )
    proj_s = (Stream(order_a, here_a, away_a), Stream(order_b, here_b, away_b))
    for s in proj_s:
        s.send()

    def advance(group, *after):
        done = list(after)
        for s in group:
            s.hold(*done)
            s.split()
            s.send()
            done = [s.away]
        return done[0]

    last = advance(proj_s, advance((expd_s, redu_s), away_a, away_b))
    last = advance((comb_s,), last)
    gh, gf = tie((grad_here, grad_far), last)
    mine, other = kernel(
        "project_back",
        project_back_kernel,
        (gh, gf, part_a, part_b, resid_grad),
        [sds(tw, F32), sds(tw, BF)],
        grid=(cols2,),
        in_specs=[lead(gh), lead(gf), lead(part_a), lead(part_b), whole(resid_grad)],
        scratch=[pltpu.VMEM(tw, F32)],
    )
    other_far = flip(other, *core_bit)
    last = other
    for _ in range(len(all_bits) - 3):
        last = advance(proj_s, advance((expd_s, redu_s), last))
        last = advance((comb_s,), last)
    input_grad = (mine + tie(other_far, last).astype(F32)).astype(BF).reshape(micro, tok, width)
    sent = to_seq(jnp.concatenate([layer_out.reshape(micro, tok, width), input_grad], axis=1))
    layer_out, input_grad = sent[:, :tok], sent[:, tok:].astype(F32)
    last = advance(proj_s, last)
    for s in streams:
        s.hold(last)
    expd_grad, redu_grad = expd_s.last(), redu_s.last()
    proj_grad = jnp.concatenate([s.last() for s in proj_s], axis=-1)
    pb = proj_grad[:, n_proj:].reshape(-1)[:n_proj]
    side = comb_s.here.shape[-1] - n_com
    places = [0] + [n_expd + v * width for v in range(6)]
    if all(place % side == 0 for place in places):
        comb_grad, eb, *vec = kernel(
            "finish",
            lambda *refs: finish_kernel([place // side for place in places], *refs),
            (comb_s.here, comb_s.got),
            [sds((i_rows, n_com), F32), sds((n_exp,), F32)] + [sds((width,), F32)] * 6,
        )
    else:
        comb_grad = comb_s.last()
        small = comb_grad[:, n_com:].reshape(-1)
        comb_grad, eb = comb_grad[:, :n_com], small[:n_exp]
        vec = [small[place : place + width] for place in places[1:]]
    return (
        layer_out,
        input_grad,
        proj_grad[:, :n_proj],
        pb,
        comb_grad,
        vec[4],
        vec[2],
        vec[3],
        expd_grad[:, :n_exp],
        eb,
        redu_grad[:, :n_exp].T,
        vec[5],
        vec[0],
        vec[1],
    )


def solution(mesh):
    placed = (
        P(None, ("row", "col"), None),
        P(None, ("row", "col"), None),
        P("row", "col"),
        P("col"),
        P("row", "col"),
        P(),
        P(),
        P(),
        P("row", "col"),
        P("col"),
        P("col", "row"),
        P(),
        P(),
        P(),
        P(),
        P(),
    )
    return jax.shard_map(
        on_device,
        mesh=mesh,
        in_specs=placed,
        out_specs=(
            P(None, ("row", "col"), None),
            P(None, ("row", "col"), None),
            P("row", "col"),
            P("col"),
            P("row", "col"),
            P(),
            P(),
            P(),
            P("row", "col"),
            P("col"),
            P("col", "row"),
            P(),
            P(),
            P(),
        ),
        check_vma=False,
    )
```
